32 devices in a mesh: ctx: 8 (over z, x), exp: 4 (over y, core).
Axes of the slice: x: 2, y: 2, z: 4, core: 2. Of those that a mesh axis runs over, the one named last changes fastest.
Arguments:
- queries: bfloat16 [2048, 4096], P('ctx', 'exp'), may hold values from -6 to 6
- keys: bfloat16 [2048, 4096], P('ctx', 'exp'), may hold values from -6 to 6
- values: bfloat16 [2048, 4096], P('ctx', 'exp'), may hold values from -6 to 6
- gates: bfloat16 [2048, 4096], P('ctx', 'exp'), may hold values from -6 to 6
- decay_rate: float32 [32], P('exp'), may hold values from 9.765625e-06 to 0.05
- norm_gain: float32 [4096], P('exp'), may hold values from 0.1 to 1.9
- moe_rows: bfloat16 [2048, 3072], P('exp'), may hold values from -6 to 6
- tile_expert: int32 [16, 1], P('exp'), may hold values from 0 to 3; in each aligned block of 4 rows (0 to 3, 4 to 7, ...) at most 2 rows name the same one
- row_weight: float32 [2048], P('exp'), may hold values from 0.2 to 1
- w_gate: bfloat16 [4, 3072, 9216], P('exp', None, 'ctx'), may hold values from -0.109375 to 0.109375
- w_up: bfloat16 [4, 3072, 9216], P('exp', None, 'ctx'), may hold values from -0.109375 to 0.109375
- w_down: bfloat16 [4, 9216, 3072], P('exp', 'ctx'), may hold values from -0.09375 to 0.09375
Outputs:
- attention_out: bfloat16 [2048, 4096], P('ctx', 'exp')
- moe_out: bfloat16 [2048, 3072], P('exp', 'ctx')
The draws below stay inside these ranges and needn't reach their ends.
Inputs may be any that keep to these rules, and one draw needn't show every extreme that they name: `tile_expert`: among the 4 tiles of one index of exp at most 2 name the same expert, and some index has exactly 2 tiles for one expert.
All inputs are finite; a program needn't handle non-finite values.
Results may differ from the reference program's by a relative error of at most 0.0057.
Values may be sent and summed in bfloat16 or wider, within the bound.
A program may use at most 128 MiB of HBM per device.

```python
import math
import jax
import jax.numpy as jnp
import numpy as np
from jax import lax

HEADS = 32
HEAD_DIM = 128
D = 3072
FFE = 9216
TILE = 128
TOK_DEV = 256
TILES_DEV = 4
CAP = 2
EXPERTS = 4
SEQ = 2048
NTILES = 16
ROWS = 2048
N_CTX = 8


def spiked(drawn, rng, source, target, parts, factor):
    owner, partner = [(jnp.arange(drawn.shape[position]) // (drawn.shape[position] // parts)).reshape([-1 if axis == position else 1 for axis in range(drawn.ndim)]) for position in (source, target)]
    chosen = jax.random.permutation(rng, parts)[partner]
    strong = (owner == chosen) | (owner == (partner + parts // 2) % parts)
    return jnp.where(strong, factor * drawn, drawn)


def block_scale(stream_key, extent, pieces, low, high):
    def one(axis_at, blocks):
        heights = jax.random.uniform(jax.random.fold_in(jax.random.fold_in(stream_key, 6), axis_at), (blocks,), jnp.float32, low / len(pieces), high / len(pieces))
        return jnp.repeat(jnp.exp(heights), extent[axis_at] // blocks).reshape((-1,) + (1,) * (len(extent) - axis_at - 1))

    factor_of = one(*pieces[0])
    for cut in pieces[1:]:
        factor_of = factor_of * one(*cut)
    return factor_of


def deal_out(key, own, number, rows, amount, top, limit, skew):
    sequence = jax.random.permutation(key, amount)
    packed, ordinary = load_shares(amount, rows * top, limit, skew, True), load_shares(amount, rows * top, limit, skew, False)
    places = jnp.arange(amount)

    def named(tallies, rotation):
        used = int((tallies > 0).sum())
        fixed = max(1, used // 4)
        moved = fixed + (places - fixed + rotation * (used - fixed)) % max(1, amount - fixed)
        return jnp.zeros((amount,), jnp.int32).at[sequence[jnp.where(places < fixed, places, moved)]].set(jnp.asarray(tallies, jnp.int32))

    tallies = jnp.where(number % 4 == 0, named(packed, number // 4), named(ordinary, number - number // 4 - 1))
    mixed = jax.random.permutation(jax.random.fold_in(own, 3), amount)
    source_of, taker = mixed[0:amount // 2 * 2:2], mixed[1:amount // 2 * 2:2]
    slack = jnp.minimum(tallies[source_of] - 1, limit - tallies[taker]) // 2
    slack = jnp.where((source_of == sequence[0]) | (taker == sequence[0]) | (tallies[taker] == 0), 0, jnp.maximum(slack, 0))
    moved = jax.random.randint(jax.random.fold_in(own, 4), (amount // 2,), 0, 1 << 20) % (slack + 1)
    tallies = tallies.at[source_of].add(-moved).at[taker].add(moved)
    items = jnp.searchsorted(jnp.cumsum(tallies), jnp.arange(rows * top), side="right").astype(jnp.int32)
    table = items.reshape(top, rows).T
    table = table[jax.random.permutation(jax.random.fold_in(own, 1), rows)]
    rotation = jax.random.randint(jax.random.fold_in(own, 2), (rows, 1), 0, top)
    return jnp.take_along_axis(table, (jnp.arange(top)[None, :] + rotation) % top, axis=1)


def load_shares(count, total, reach, slope, full):
    portions = [(1 << 20) // math.isqrt(rank ** slope) + 1 for rank in range(1, count + 1)]
    largest = reach if full else min(reach, max(-(-total // count), total * portions[0] // sum(portions)))
    least = 1 if total - largest >= count - 1 else 0
    given, rest = [largest] + [least] * (count - 1), total - largest - least * (count - 1)
    while rest > 0:
        candidates = [i for i in range(1, count) if given[i] < largest] or [i for i in range(1, count) if given[i] < reach]
        whole, left = sum([portions[i] for i in candidates]), rest
        for i in candidates:
            more = min(reach - given[i], max(1, left * portions[i] // whole), rest)
            given[i] = given[i] + more
            rest = rest - more
    return np.array(given)


def centred(own_key, extent, deviation, reach, cuts=(), kind=jnp.bfloat16):
    values = jax.random.normal(own_key, extent, jnp.float32) * deviation
    if len(cuts) > 0:
        values = block_scale(own_key, extent, cuts, -0.22, 0.18) * values
    return jnp.clip(values, min=-reach, max=reach).astype(kind)


def heavy_noise(own_key, extent, deviation, limit, split, heavy, kind=jnp.bfloat16):
    values = deviation * jax.random.normal(own_key, extent, jnp.float32)
    if split:
        values = values * block_scale(own_key, extent, split, -0.22, 0.18)
    return jnp.clip(spiked(values, jax.random.fold_in(own_key, 3), *heavy), -limit, limit).astype(kind)


def setup_inputs(seed: int = 0) -> dict:
    splits = jax.random.split(jax.random.key(seed), 13)
    queries = centred(splits[0], (SEQ, HEADS * HEAD_DIM), 1.0, 6.0, ((0, 8), (1, 4)))
    keys = centred(splits[1], (SEQ, HEADS * HEAD_DIM), 1.0, 6.0, ((0, 8), (1, 4)))
    values = centred(splits[2], (SEQ, HEADS * HEAD_DIM), 1.0, 6.0, ((0, 8), (1, 4)))
    gates = centred(splits[3], (SEQ, HEADS * HEAD_DIM), 1.5, 6.0, ((0, 8), (1, 4)))
    decay_rate = jnp.clip(jnp.exp(math.log(0.05) - 8.54091 * jax.random.uniform(splits[4], (HEADS,), jnp.float32) ** block_scale(splits[4], (HEADS,), ((0, 4),), -0.2, 0.2)), 9.765624781721272e-06, 0.05)
    norm_gain = jnp.clip(1.0 + 0.18 * jax.random.normal(splits[5], (HEADS * HEAD_DIM,), jnp.float32), 0.1, 1.9)
    moe_rows = centred(splits[6], (ROWS, D), 1.0, 6.0, ((0, 4),))
    tile_expert_keys = jax.random.split(jax.random.fold_in(splits[7], 1), NTILES // TILES_DEV)
    tile_expert_turns = jax.random.permutation(jax.random.fold_in(splits[7], 3), NTILES // TILES_DEV)
    tile_expert = jax.vmap(lambda own, number: deal_out(jax.random.fold_in(splits[7], 2), own, number, TILES_DEV, EXPERTS, 1, CAP, 2))(tile_expert_keys, tile_expert_turns).reshape((NTILES, 1))
    row_weight = jnp.clip(0.2 + 0.8 * jax.random.uniform(splits[8], (ROWS,), jnp.float32) ** block_scale(splits[8], (ROWS,), ((0, 4),), -0.2, 0.2), 0.2, 1.0)
    w_gate = centred(splits[9], (EXPERTS, D, FFE), D ** -0.5, 0.109375, ((0, 4), (2, 8)))
    w_up = centred(splits[10], (EXPERTS, D, FFE), D ** -0.5, 0.109375, ((0, 4), (2, 8)))
    w_down = heavy_noise(splits[11], (EXPERTS, FFE, D), FFE ** -0.5, 0.09375, ((0, 4), (1, 8)), (1, 2, 8, 2.0))
    return dict(queries=queries, keys=keys, values=values, gates=gates, decay_rate=decay_rate, norm_gain=norm_gain, moe_rows=moe_rows, tile_expert=tile_expert, row_weight=row_weight, w_gate=w_gate, w_up=w_up, w_down=w_down)


def attention_part(queries, keys, values, gates, decay_rate, norm_gain):
    positions = jnp.arange(TOK_DEV, dtype=jnp.float32)
    offsets = positions[:, None] - positions[None, :]
    within = jnp.exp(-decay_rate[:, None, None] * jnp.maximum(offsets, 0.0)[None])
    within = jnp.where((offsets >= 0.0)[None], within, 0.0)
    query_decay = jnp.exp(-decay_rate[None, :] * positions[:, None])
    key_decay = jnp.exp(-decay_rate[None, :] * (TOK_DEV - positions)[:, None])
    block_decay = jnp.exp(-decay_rate * TOK_DEV)
    shape_blocks = (N_CTX, TOK_DEV, HEADS, HEAD_DIM)
    query_blocks = queries.reshape(shape_blocks)
    key_blocks = keys.reshape(shape_blocks)
    value_blocks = values.reshape(shape_blocks)

    def one_block(prefix, block):
        query_heads, key_heads, value_heads = block
        query_wide = query_heads.astype(jnp.float32)
        key_wide = key_heads.astype(jnp.float32)
        value_wide = value_heads.astype(jnp.float32)
        scores = (jnp.einsum('the,she->hts', query_wide, key_wide) * within).astype(jnp.bfloat16)
        intra = jnp.einsum('hts,she->the', scores.astype(jnp.float32), value_wide)
        prefix_low = prefix.astype(jnp.bfloat16).astype(jnp.float32)
        inter = jnp.einsum('the,hef->thf', query_wide, prefix_low) * query_decay[:, :, None]
        key_scaled = (key_wide * key_decay[:, :, None]).astype(jnp.bfloat16)
        local_state = jnp.einsum('the,thf->hef', key_scaled.astype(jnp.float32), value_wide)
        next_prefix = prefix * block_decay[:, None, None] + local_state
        return (next_prefix, intra + inter)
    start_state = jnp.zeros((HEADS, HEAD_DIM, HEAD_DIM), jnp.float32)
    final_state, mixed = lax.scan(one_block, start_state, (query_blocks, key_blocks, value_blocks))
    mixed = mixed.reshape(SEQ, HEADS * HEAD_DIM)
    mean_square = lax.optimization_barrier(jnp.mean(mixed * mixed, axis=1))
    scaled = mixed * lax.rsqrt(mean_square + 1e-06)[:, None] * norm_gain[None, :]
    return (scaled * jax.nn.sigmoid(gates.astype(jnp.float32))).astype(jnp.bfloat16)

def expert_part(moe_rows, tile_expert, row_weight, w_gate, w_up, w_down):
    row_tiles = moe_rows.reshape(NTILES, TILE, D)
    tile_ids = tile_expert[:, 0].astype(jnp.int32)

    def one_tile(pair):
        rows, which = pair
        gate_matrix = lax.dynamic_index_in_dim(w_gate, which, 0, keepdims=False)
        up_matrix = lax.dynamic_index_in_dim(w_up, which, 0, keepdims=False)
        down_matrix = lax.dynamic_index_in_dim(w_down, which, 0, keepdims=False)
        gate_part = jnp.dot(rows, gate_matrix, preferred_element_type=jnp.float32)
        up_part = jnp.dot(rows, up_matrix, preferred_element_type=jnp.float32)
        hidden = (jax.nn.silu(gate_part) * up_part).astype(jnp.bfloat16)
        return jnp.dot(hidden, down_matrix, preferred_element_type=jnp.float32).astype(jnp.bfloat16)
    expert_out = lax.map(one_tile, (row_tiles, tile_ids))
    expert_out = lax.optimization_barrier(expert_out)
    weighted = expert_out.astype(jnp.float32) * row_weight.reshape(NTILES, TILE)[:, :, None]
    return weighted.astype(jnp.bfloat16).reshape(ROWS, D)

def reference(queries, keys, values, gates, decay_rate, norm_gain, moe_rows, tile_expert, row_weight, w_gate, w_up, w_down):
    attention_out = attention_part(queries, keys, values, gates, decay_rate, norm_gain)
    moe_out = expert_part(moe_rows, tile_expert, row_weight, w_gate, w_up, w_down)
    return (attention_out, moe_out)
```

```python
import functools

import jax
import jax.numpy as jnp
from jax import lax
from jax.experimental import pallas as pl
from jax.experimental.pallas import tpu as pltpu
from jax.sharding import PartitionSpec as P

MESH = pl.DeviceIdType.MESH
CHUNKS = 8


def carried_state(local_state, decay_rate, tokens_here):
    peers, mine = (lax.axis_size("ctx"), lax.axis_index("ctx"))
    everything = lax.all_gather(local_state.astype(jnp.bfloat16), "ctx")
    distance = (mine - 1 - jnp.arange(peers)).astype(jnp.float32)
    weight = jnp.exp(-decay_rate[None, :] * tokens_here * jnp.maximum(distance, 0.0)[:, None])
    weight = jnp.where((distance >= 0.0)[:, None], weight, 0.0)
    return jnp.sum(everything.astype(jnp.float32) * weight[:, :, None, None], axis=0)


def attention_part(queries, keys, values, gates, decay_rate, norm_gain):
    tokens_here = queries.shape[0]
    heads_here = decay_rate.shape[0]
    head_width = queries.shape[1] // heads_here
    query_heads = queries.reshape(tokens_here, heads_here, head_width)
    key_heads = keys.reshape(tokens_here, heads_here, head_width)
    value_heads = values.reshape(tokens_here, heads_here, head_width)
    positions = jnp.arange(tokens_here, dtype=jnp.float32)
    offsets = positions[:, None] - positions[None, :]
    within = jnp.exp(-decay_rate[:, None, None] * jnp.maximum(offsets, 0.0)[None])
    within = jnp.where((offsets >= 0.0)[None], within, 0.0)
    query_decay = jnp.exp(-decay_rate[None, :] * positions[:, None])
    key_decay = jnp.exp(-decay_rate[None, :] * (tokens_here - positions)[:, None])
    key_scaled = (key_heads.astype(jnp.float32) * key_decay[:, :, None]).astype(jnp.bfloat16)
    local_state = jnp.einsum(
        "the,thf->hef", key_scaled, value_heads, preferred_element_type=jnp.float32
    )
    prefix = carried_state(local_state, decay_rate, tokens_here)
    scores = jnp.einsum("the,she->hts", query_heads, key_heads, preferred_element_type=jnp.float32)
    scores = (scores * within).astype(jnp.bfloat16)
    intra = jnp.einsum("hts,she->the", scores, value_heads, preferred_element_type=jnp.float32)
    inter = jnp.einsum(
        "the,hef->thf", query_heads, prefix.astype(jnp.bfloat16), preferred_element_type=jnp.float32
    )
    mixed = (intra + inter * query_decay[:, :, None]).reshape(tokens_here, heads_here * head_width)
    square_part = jnp.sum(mixed * mixed, axis=1)
    square_total = lax.psum(square_part, "exp")
    mean_square = square_total / (heads_here * head_width * lax.axis_size("exp"))
    scaled = mixed * lax.rsqrt(mean_square + 1e-06)[:, None] * norm_gain[None, :]
    return (scaled * jax.nn.sigmoid(gates.astype(jnp.float32))).astype(jnp.bfloat16)


def chunk_mask(t):
    late = t // 4
    return (1 - late) * (t // 2) + late * (2 + t % 2)


def chunk_slot(t):
    late = t // 4
    return (1 - late) * (t % 2) + late * ((t - 4) // 2)


def flipped(me, mask):
    low, high = me % 2, (me // 2) % 2
    return me + (mask % 2) * (1 - 2 * low) + 2 * (mask // 2) * (1 - 2 * high)


def pick_kernel(index_ref, tile_ref, out_ref):
    out_ref[...] = tile_ref[...]


def pick_tiles(row_tiles, index):
    tile_len, width = row_tiles.shape[1:]
    return pl.pallas_call(
        pick_kernel,
        grid_spec=pltpu.PrefetchScalarGridSpec(
            num_scalar_prefetch=1,
            grid=(CHUNKS,),
            in_specs=[pl.BlockSpec((1, tile_len, width), lambda t, index: (index[t], 0, 0))],
            out_specs=pl.BlockSpec((1, tile_len, width), lambda t, index: (t, 0, 0)),
        ),
        out_shape=jax.ShapeDtypeStruct((CHUNKS, tile_len, width), row_tiles.dtype),
        name="pick_tiles",
    )(index, row_tiles)


def expert_kernel(
    groups,
    send_ref,
    gate_hbm,
    up_hbm,
    down_hbm,
    rate_ref,
    query_ref,
    key_ref,
    value_ref,
    gates_ref,
    gain_ref,
    out_ref,
    mixed_ref,
    gate_w,
    up_w,
    down_w,
    arrived,
    hidden,
    kept,
    pair_out,
    pair_in,
    group_out,
    group_in,
    result,
    back,
    weight_sem,
    own_sem,
    give_send,
    give_recv,
    pair_send,
    pair_recv,
    group_send,
    group_recv,
    back_send,
    back_recv,
    mixed,
    state,
    state_out,
    state_in,
    chain_out,
    chain_in,
    prefix,
    square_out,
    square_in,
    state_sem,
    chain_sem,
    square_send,
    square_recv,
):
    row, col = lax.axis_index("ctx"), lax.axis_index("exp")
    half, group = row % 2, row // 2
    partner = row + 1 - 2 * half
    wide = kept.shape[-1]
    peers = [(row, flipped(col, mask)) for mask in (1, 2, 3)] + [(partner, col)]
    peers += [(((group + j) % groups) * 2 + half, col) for j in range(1, groups)]

    weights = [
        pltpu.make_async_copy(gate_hbm.at[0], gate_w, weight_sem.at[0]),
        pltpu.make_async_copy(up_hbm.at[0], up_w, weight_sem.at[1]),
        pltpu.make_async_copy(down_hbm.at[0], down_w, weight_sem.at[2]),
    ]
    own = [
        pltpu.make_async_copy(send_ref.at[t], arrived.at[t], own_sem.at[t]) for t in range(2)
    ]

    barrier = pltpu.get_barrier_semaphore()
    for peer in peers:
        pl.semaphore_signal(barrier, inc=1, device_id=peer, device_id_type=MESH)
    for copy in own + weights:
        copy.start()
    pl.semaphore_wait(barrier, len(peers))

    def give(t):
        return pltpu.make_async_remote_copy(
            src_ref=send_ref.at[t],
            dst_ref=arrived.at[t],
            send_sem=give_send.at[t],
            recv_sem=give_recv.at[t],
            device_id=(row, flipped(col, chunk_mask(t))),
            device_id_type=MESH,
        )

    def pair(t):
        return pltpu.make_async_remote_copy(
            src_ref=pair_out.at[t],
            dst_ref=pair_in.at[t],
            send_sem=pair_send.at[t],
            recv_sem=pair_recv.at[t],
            device_id=(partner, col),
            device_id_type=MESH,
        )

    def spread(t, j):
        target = (group + j) % groups
        return pltpu.make_async_remote_copy(
            src_ref=group_out.at[t, target],
            dst_ref=group_in.at[t, j],
            send_sem=group_send.at[t, j],
            recv_sem=group_recv.at[t, j],
            device_id=(target * 2 + half, col),
            device_id_type=MESH,
        )

    def home(t):
        return pltpu.make_async_remote_copy(
            src_ref=result.at[t],
            dst_ref=back.at[t],
            send_sem=back_send.at[t],
            recv_sem=back_recv.at[t],
            device_id=(row, flipped(col, chunk_mask(t))),
            device_id_type=MESH,
        )

    for t in (2, 3, 4, 5, 6, 7):
        give(t).start()

    tokens, features = query_ref.shape
    heads, size = state.shape[0], state.shape[1]
    place = lax.broadcasted_iota(jnp.int32, (tokens, size), 0).astype(jnp.float32)

    def lanes(h):
        return pl.ds(pl.multiple_of(h * size, 128), size)

    def fill(value):
        return jnp.exp(jnp.full((size, size), value, jnp.float32))

    swap = pltpu.make_async_remote_copy(
        src_ref=state_out,
        dst_ref=state_in,
        send_sem=state_sem.at[0],
        recv_sem=state_sem.at[1],
        device_id=(partner, col),
        device_id_type=MESH,
    )
    chain = pltpu.make_async_remote_copy(
        src_ref=chain_out,
        dst_ref=chain_in,
        send_sem=chain_sem.at[0],
        recv_sem=chain_sem.at[1],
        device_id=(((group + 1) % groups) * 2 + half, col),
        device_id_type=MESH,
    )

    def square(j):
        return pltpu.make_async_remote_copy(
            src_ref=square_out,
            dst_ref=square_in.at[j],
            send_sem=square_send.at[j],
            recv_sem=square_recv.at[j],
            device_id=(row, flipped(col, j)),
            device_id_type=MESH,
        )

    def local(h, carry):
        decay = jnp.exp(-rate_ref[h] * (tokens - place))
        scaled = (key_ref[:, lanes(h)].astype(jnp.float32) * decay).astype(jnp.bfloat16)
        found = lax.dot_general(
            scaled,
            value_ref[:, lanes(h)],
            (((0,), (0,)), ((), ())),
            preferred_element_type=jnp.float32,
        )
        state[h] = found
        state_out[h] = found.astype(jnp.bfloat16)
        return carry

    lax.fori_loop(0, heads, local, 0)
    swap.start()

    def intra(h):
        offset = lax.broadcasted_iota(jnp.int32, (tokens, tokens), 0) - lax.broadcasted_iota(
            jnp.int32, (tokens, tokens), 1
        )
        gap = jnp.maximum(offset, 0).astype(jnp.float32)
        within = jnp.where(offset >= 0, jnp.exp(-rate_ref[h] * gap), 0.0)
        scores = lax.dot_general(
            query_ref[:, lanes(h)],
            key_ref[:, lanes(h)],
            (((1,), (1,)), ((), ())),
            preferred_element_type=jnp.float32,
        )
        scores = (scores * within).astype(jnp.bfloat16)
        mixed[:, lanes(h)] = jnp.dot(
            scores, value_ref[:, lanes(h)], preferred_element_type=jnp.float32
        )

    def carry_on():
        @pl.when(group > 0)
        def _():
            chain.wait_recv()

        @pl.when(group == 0)
        def _():
            prefix[...] = jnp.zeros_like(prefix)

        @pl.when(group > 0)
        def _():
            prefix[...] = chain_in[...].astype(jnp.float32)

        first = (half == 0).astype(jnp.float32)

        def one(h, carry):
            decay = fill(-rate_ref[h] * tokens)
            mine, other, before = state[h], state_in[h].astype(jnp.float32), prefix[h]
            early = first * mine + (1.0 - first) * other
            late = first * other + (1.0 - first) * mine
            middle = before * decay + early
            chain_out[h] = (middle * decay + late).astype(jnp.bfloat16)
            prefix[h] = first * before + (1.0 - first) * middle
            return carry

        lax.fori_loop(0, heads, one, 0)

        @pl.when(group < groups - 1)
        def _():
            chain.start()

    def join():
        squares = jnp.zeros((tokens, size), jnp.float32)
        for h in range(heads):
            cut = slice(h * size, (h + 1) * size)
            inter = jnp.dot(
                query_ref[:, cut],
                prefix[h].astype(jnp.bfloat16),
                preferred_element_type=jnp.float32,
            )
            both = mixed[:, cut] + inter * jnp.exp(-rate_ref[h] * place)
            mixed[:, cut] = both
            squares = squares + both * both
        square_out[...] = squares
        for j in (1, 2, 3):
            square(j).start()

    for copy in own + weights:
        copy.wait()

    def step(t, carry):
        @pl.when(t < CHUNKS)
        def _():
            @pl.when(t >= 2)
            def _():
                give(t).wait_recv()

            span = 384 if hidden.shape[1] % 384 == 0 else 128
            for start in range(0, hidden.shape[1], span):
                cut = pl.ds(start, span)
                rows = arrived[t]
                gated = jnp.dot(rows, gate_w[:, cut], preferred_element_type=jnp.float32)
                raised = jnp.dot(rows, up_w[:, cut], preferred_element_type=jnp.float32)
                hidden[:, cut] = (jax.nn.silu(gated) * raised).astype(jnp.bfloat16)
            for g in range(groups):
                theirs = pl.ds(pl.multiple_of((2 * g + 1 - half) * wide, 128), wide)
                pair_out[t, g] = jnp.dot(
                    hidden[...], down_w[:, theirs], preferred_element_type=jnp.float32
                ).astype(jnp.bfloat16)
            pair(t).start()

            @pl.when(t < heads)
            def _():
                intra(t)

            for g in range(groups):
                mine = pl.ds(pl.multiple_of((2 * g + half) * wide, 128), wide)
                kept[t, g] = jnp.dot(
                    hidden[...], down_w[:, mine], preferred_element_type=jnp.float32
                )

        @pl.when((t >= 1) & (t < CHUNKS + 1))
        def _():
            u = t - 1
            pair(u).wait_recv()
            for g in range(groups):
                total = kept[u, g] + pair_in[u, g].astype(jnp.float32)
                kept[u, g] = total
                group_out[u, g] = total.astype(jnp.bfloat16)
            for j in range(1, groups):
                spread(u, j).start()

        @pl.when(t == 1)
        def _():
            swap.wait_recv()

        @pl.when(t == 1 + group)
        def _():
            carry_on()

        @pl.when(t == CHUNKS)
        def _():
            join()

        @pl.when(t >= 2)
        def _():
            u = t - 2
            total = kept[u, group]
            for j in range(1, groups):
                spread(u, j).wait_recv()
                total = total + group_in[u, j].astype(jnp.float32)
            result[u] = total.astype(jnp.bfloat16)

            @pl.when(u >= 2)
            def _():
                home(u).start()

        return carry

    lax.fori_loop(0, CHUNKS + 2, step, 0)

    squares = square_out[...]
    for j in (1, 2, 3):
        square(j).wait_recv()
        squares = squares + square_in[j]
    mean = jnp.sum(squares, axis=1, keepdims=True) / (features * 4)
    scale = lax.rsqrt(mean + 1e-06)
    for h in range(heads):
        cut = slice(h * size, (h + 1) * size)
        gate = jax.nn.sigmoid(gates_ref[:, cut].astype(jnp.float32))
        mixed_ref[:, cut] = (mixed[:, cut] * scale * gain_ref[:, cut] * gate).astype(jnp.bfloat16)
    swap.wait_send()

    @pl.when(group < groups - 1)
    def _():
        chain.wait_send()

    for j in (1, 2, 3):
        square(j).wait_send()
    for t in range(2):
        out_ref[t] = result[t]
    for t in range(CHUNKS):
        pair(t).wait_send()
        for j in range(1, groups):
            spread(t, j).wait_send()
    for t in range(2, CHUNKS):
        give(t).wait_send()
        home(t).wait_send()
        home(t).wait_recv()
        out_ref[t] = back[t]


def expert_call(send_buffer, w_gate, w_up, w_down, column_count, attention):
    tile_len, width = send_buffer.shape[1:]
    units = w_gate.shape[2]
    groups = lax.axis_size("ctx") // 2
    low, wide = jnp.bfloat16, jnp.float32
    block = (tile_len, column_count)
    dma = pltpu.SemaphoreType.DMA
    queries, keys, values, gates, decay_rate, norm_gain = attention
    tokens, heads = queries.shape[0], decay_rate.shape[0]
    size = queries.shape[1] // heads
    vmem = pl.BlockSpec(memory_space=pltpu.VMEM)
    return pl.pallas_call(
        functools.partial(expert_kernel, groups),
        out_shape=(
            jax.ShapeDtypeStruct((CHUNKS,) + block, low),
            jax.ShapeDtypeStruct(queries.shape, low),
        ),
        in_specs=[pl.BlockSpec(memory_space=pl.ANY)] * 4
        + [pl.BlockSpec(memory_space=pltpu.SMEM)]
        + [vmem] * 5,
        out_specs=(vmem, vmem),
        scratch_shapes=[
            pltpu.VMEM((width, units), low),
            pltpu.VMEM((width, units), low),
            pltpu.VMEM((units, width), low),
            pltpu.VMEM((CHUNKS, tile_len, width), low),
            pltpu.VMEM((tile_len, units), low),
            pltpu.VMEM((CHUNKS, groups) + block, wide),
            pltpu.VMEM((CHUNKS, groups) + block, low),
            pltpu.VMEM((CHUNKS, groups) + block, low),
            pltpu.VMEM((CHUNKS, groups) + block, low),
            pltpu.VMEM((CHUNKS, groups) + block, low),
            pltpu.VMEM((CHUNKS,) + block, low),
            pltpu.VMEM((CHUNKS,) + block, low),
            dma((3,)),
            dma((2,)),
            dma((CHUNKS,)),
            dma((CHUNKS,)),
            dma((CHUNKS,)),
            dma((CHUNKS,)),
            dma((CHUNKS, groups)),
            dma((CHUNKS, groups)),
            dma((CHUNKS,)),
            dma((CHUNKS,)),
            pltpu.VMEM(queries.shape, wide),
            pltpu.VMEM((heads, size, size), wide),
            pltpu.VMEM((heads, size, size), low),
            pltpu.VMEM((heads, size, size), low),
            pltpu.VMEM((heads, size, size), low),
            pltpu.VMEM((heads, size, size), low),
            pltpu.VMEM((heads, size, size), wide),
            pltpu.VMEM((tokens, size), wide),
            pltpu.VMEM((4, tokens, size), wide),
            dma((2,)),
            dma((2,)),
            dma((4,)),
            dma((4,)),
        ],
        compiler_params=pltpu.CompilerParams(
            collective_id=0, has_side_effects=True, vmem_limit_bytes=62 * 1024 * 1024
        ),
        cost_estimate=pl.CostEstimate(
            flops=6 * CHUNKS * tile_len * width * units,
            bytes_accessed=300_000_000,
            transcendentals=0,
        ),
        name="expert_tiles",
    )(
        send_buffer, w_gate, w_up, w_down,
        decay_rate, queries, keys, values, gates, norm_gain[None, :],
    )


SLOTS = 5
PARTS = 4


def fast_kernel(
    ids_ref,
    rate_ref,
    rows_hbm,
    gate_hbm,
    up_hbm,
    down_hbm,
    query_hbm,
    key_hbm,
    value_hbm,
    gates_hbm,
    gain_hbm,
    out_ref,
    mixed_ref,
    spill_ref,
    ids,
    raw,
    gate_w,
    up_w,
    down_w,
    query,
    key,
    value,
    gates,
    gain,
    rows,
    straight_out,
    core_out,
    diag_out,
    seconds,
    extra,
    hidden,
    kept,
    x_out,
    x_in,
    near_out,
    near_in,
    far_out,
    far_in,
    result,
    back,
    mixed,
    state,
    state_out,
    state_in,
    chain_out,
    chain_in,
    prefix,
    square_out,
    square_in,
    load_sem,
    give_sem,
    x_sem,
    near_sem,
    far_sem,
    home_sem,
    state_sem,
    chain_sem,
    square_sem,
):
    row, col = lax.axis_index("ctx"), lax.axis_index("exp")
    half, z = row % 2, row // 2
    core, odd = col % 2, z % 2
    partner = row + 1 - 2 * half
    near = z + 1 - 2 * odd
    far, cross = (z + 2) % PARTS, (near + 2) % PARTS
    order = (cross, near, far, z)
    tiles, tile_len = raw.shape[0], raw.shape[1]
    wide = kept.shape[-1]
    units = hidden.shape[1]
    span = units // 3
    half_len, piece = tile_len // 2, tile_len // 4

    def line(other):
        return (other * 2 + half, col)

    def mate(mask):
        return (row, flipped(col, mask))

    def load(source, target, number):
        return pltpu.make_async_copy(source, target, load_sem.at[number])

    def weight_cut(number):
        cut = pl.ds(number * span, span)
        return [
            load(gate_hbm.at[0, :, cut], gate_w.at[:, cut], 4 + 2 * number),
            load(up_hbm.at[0, :, cut], up_w.at[:, cut], 5 + 2 * number),
        ]

    key_load, value_load = load(key_hbm, key, 0), load(value_hbm, value, 1)
    query_load, rows_load = load(query_hbm, query, 2), load(rows_hbm, raw, 3)
    down_load = load(down_hbm.at[0], down_w, 10)
    gates_load, gain_load = load(gates_hbm, gates, 11), load(gain_hbm, gain, 12)

    peers = [mate(mask) for mask in (1, 2, 3)] + [(partner, col)]
    peers += [line(other) for other in (near, far, cross)]
    barrier = pltpu.get_barrier_semaphore()
    for peer in peers:
        pl.semaphore_signal(barrier, inc=1, device_id=peer, device_id_type=MESH)
    for copy in [key_load, value_load, rows_load] + weight_cut(0) + weight_cut(1) + weight_cut(2):
        copy.start()
    for copy in (down_load, query_load, gates_load, gain_load):
        copy.start()

    def remote(source, target, sems, place, device):
        return pltpu.make_async_remote_copy(
            src_ref=source,
            dst_ref=target,
            send_sem=sems.at[(0,) + place],
            recv_sem=sems.at[(1,) + place],
            device_id=device,
            device_id_type=MESH,
        )

    my_core = pl.ds(pl.multiple_of(core * half_len, 32), half_len)

    def my_piece(i):
        return pl.ds(pl.multiple_of(odd * half_len + i * piece, 32), piece)

    def give_ids(mask):
        return remote(ids_ref, ids.at[mask], give_sem, (8 + mask,), mate(mask))

    give_core = remote(core_out, rows.at[1], give_sem, (0,), mate(1))
    give_second = remote(seconds.at[0], seconds.at[1], give_sem, (1,), mate(1))
    give_diag = remote(diag_out, rows.at[4], give_sem, (8,), mate(3))
    give_extra = remote(
        extra.at[0, my_core], extra.at[1, my_core], give_sem, (6,), mate(2)
    )
    pass_extra = remote(
        extra.at[1, my_core], extra.at[1, my_core], give_sem, (7,), mate(1)
    )

    def give_straight(i):
        return remote(
            straight_out.at[pl.ds(i * piece, piece)],
            rows.at[2, my_piece(i)],
            give_sem,
            (2 + i,),
            mate(2),
        )

    def pass_straight(i):
        return remote(
            rows.at[2, my_piece(i)], rows.at[2, my_piece(i)], give_sem, (4 + i,), line(near)
        )

    def across(t, j):
        cut = pl.ds(2 * j, 2)
        return remote(x_out.at[t, cut], x_in.at[t, cut], x_sem, (t, j), (partner, col))

    def along_near(t):
        return remote(near_out.at[t], near_in.at[t], near_sem, (t,), line(near))

    def along_far(t):
        return remote(far_out.at[t], far_in.at[t], far_sem, (t,), line(far))

    def home(t, mask, slot):
        return remote(result.at[t], back.at[slot], home_sem, (slot,), mate(mask))

    swap = remote(state_out, state_in, state_sem, (), (partner, col))
    chain = remote(chain_out, chain_in, chain_sem, (), line((z + 1) % PARTS))

    def square(j):
        return remote(square_out, square_in.at[j], square_sem, (j,), mate(j))

    def first_of(expert):
        found = jnp.int32(0)
        for t in reversed(range(tiles)):
            found = jnp.where(ids_ref[t, 0] == expert, t, found)
        return found

    def repeats(read):
        seen = []
        for t in range(tiles):
            again = jnp.int32(0)
            for u in range(t):
                again = jnp.where(read(u) == read(t), 1, again)
            seen.append(again)
        return seen

    own_again = repeats(lambda t: ids_ref[t, 0])

    tokens, features = query.shape
    heads, size = state.shape[0], state.shape[1]
    place = lax.broadcasted_iota(jnp.int32, (tokens, size), 0).astype(jnp.float32)

    def lanes(h):
        return pl.ds(pl.multiple_of(h * size, 128), size)

    def fill(number):
        return jnp.exp(jnp.full((size, size), number, jnp.float32))

    key_load.wait()
    value_load.wait()

    def local(h, carry):
        decay = jnp.exp(-rate_ref[h] * (tokens - place))
        scaled = (key[:, lanes(h)].astype(jnp.float32) * decay).astype(jnp.bfloat16)
        found = lax.dot_general(
            scaled,
            value[:, lanes(h)],
            (((0,), (0,)), ((), ())),
            preferred_element_type=jnp.float32,
        )
        state[h] = found
        state_out[h] = found.astype(jnp.bfloat16)
        return carry

    lax.fori_loop(0, heads, local, 0)
    for t in range(tiles):
        ids[0, t, 0] = ids_ref[t, 0]
    rows_load.wait()
    my_half = pl.ds(pl.multiple_of(odd * half_len, 32), half_len)
    straight_out[...] = raw[first_of(flipped(col, 2)), my_half, :]

    pl.semaphore_wait(barrier, len(peers))
    for i in range(2):
        give_straight(i).start()
    swap.start()
    core_out[...] = raw[first_of(flipped(col, 1))]
    give_core.start()
    second = jnp.int32(0)
    for t in range(tiles):
        second = jnp.where(own_again[t] == 1, t, second)
    seconds[0] = raw[second]
    give_second.start()
    for mask in (1, 2, 3):
        give_ids(mask).start()
    rows[0] = raw[first_of(col)]
    diag_out[...] = raw[first_of(flipped(col, 3))]

    def intra(h):
        offset = lax.broadcasted_iota(jnp.int32, (tokens, tokens), 0) - lax.broadcasted_iota(
            jnp.int32, (tokens, tokens), 1
        )
        gap = jnp.maximum(offset, 0).astype(jnp.float32)
        within = jnp.where(offset >= 0, jnp.exp(-rate_ref[h] * gap), 0.0)
        scores = lax.dot_general(
            query[:, lanes(h)],
            key[:, lanes(h)],
            (((1,), (1,)), ((), ())),
            preferred_element_type=jnp.float32,
        )
        scores = (scores * within).astype(jnp.bfloat16)
        mixed[:, lanes(h)] = jnp.dot(scores, value[:, lanes(h)], preferred_element_type=jnp.float32)

    def carry_on():
        @pl.when(z > 0)
        def _():
            chain.wait_recv()
            prefix[...] = chain_in[...].astype(jnp.float32)

        @pl.when(z == 0)
        def _():
            prefix[...] = jnp.zeros_like(prefix)

        first = (half == 0).astype(jnp.float32)

        def one(h, carry):
            decay = fill(-rate_ref[h] * tokens)
            mine, other, before = state[h], state_in[h].astype(jnp.float32), prefix[h]
            early = first * mine + (1.0 - first) * other
            late = first * other + (1.0 - first) * mine
            middle = before * decay + early
            chain_out[h] = (middle * decay + late).astype(jnp.bfloat16)
            prefix[h] = first * before + (1.0 - first) * middle
            return carry

        lax.fori_loop(0, heads, one, 0)

        @pl.when(z < PARTS - 1)
        def _():
            chain.start()

    def join():
        squares = jnp.zeros((tokens, size), jnp.float32)
        for h in range(heads):
            cut = slice(h * size, (h + 1) * size)
            inter = jnp.dot(
                query[:, cut], prefix[h].astype(jnp.bfloat16), preferred_element_type=jnp.float32
            )
            both = mixed[:, cut] + inter * jnp.exp(-rate_ref[h] * place)
            mixed[:, cut] = both
            squares = squares + both * both
        square_out[...] = squares
        for j in (1, 2, 3):
            square(j).start()

    def finish():
        gates_load.wait()
        gain_load.wait()
        squares = square_out[...]
        for j in (1, 2, 3):
            square(j).wait_recv()
            squares = squares + square_in[j]
        mean = jnp.sum(squares, axis=1, keepdims=True) / (features * 4)
        scale = lax.rsqrt(mean + 1e-06)
        for h in range(heads):
            cut = slice(h * size, (h + 1) * size)
            gate = jax.nn.sigmoid(gates[:, cut].astype(jnp.float32))
            mixed_ref[:, cut] = (mixed[:, cut] * scale * gain[:, cut] * gate).astype(jnp.bfloat16)

    def compute(t):
        for number in range(3):
            cut = pl.ds(number * span, span)

            @pl.when(t == 0)
            def _():
                for copy in weight_cut(number):
                    copy.wait()

            tile = rows[t]
            gated = jnp.dot(tile, gate_w[:, cut], preferred_element_type=jnp.float32)
            raised = jnp.dot(tile, up_w[:, cut], preferred_element_type=jnp.float32)
            hidden[:, cut] = (jax.nn.silu(gated) * raised).astype(jnp.bfloat16)

        @pl.when(t == 0)
        def _():
            down_load.wait()

        def block(part, side):
            cut = pl.ds(pl.multiple_of((2 * order[part] + side) * wide, 128), wide)
            return jnp.dot(hidden[...], down_w[:, cut], preferred_element_type=jnp.float32)

        for j in range(2):
            for part in (2 * j, 2 * j + 1):
                x_out[t, part] = block(part, 1 - half).astype(jnp.bfloat16)
            across(t, j).start()
        for part in range(PARTS):
            kept[t, part] = block(part, half)

    def take_x(u):
        across(u, 0).wait_recv()
        for part in range(2):
            total = kept[u, part] + x_in[u, part].astype(jnp.float32)
            near_out[u, part] = total.astype(jnp.bfloat16)
        along_near(u).start()
        across(u, 1).wait_recv()
        for part in (2, 3):
            kept[u, part] = kept[u, part] + x_in[u, part].astype(jnp.float32)

    def take_near(u):
        along_near(u).wait_recv()
        far_out[u] = (kept[u, 2] + near_in[u, 0].astype(jnp.float32)).astype(jnp.bfloat16)
        along_far(u).start()
        kept[u, 3] = kept[u, 3] + near_in[u, 1].astype(jnp.float32)

    def take_far(u):
        along_far(u).wait_recv()
        done = (kept[u, 3] + far_in[u].astype(jnp.float32)).astype(jnp.bfloat16)
        result[u] = done

        @pl.when(u == 0)
        def _():
            back[0] = done

        @pl.when(u == 1)
        def _():
            home(u, 1, 1).start()

        @pl.when(u == 2)
        def _():
            home(u, 2, 2).start()

        @pl.when(u == 3)
        def _():
            for mask in (1, 2, 3):
                home(u, mask, 4 + mask).start()
            back[4] = done

        @pl.when(u == 4)
        def _():
            home(u, 3, 3).start()

    def step(t, carry):
        @pl.when(t == 2)
        def _():
            for i in range(2):
                pass_straight(i).wait_recv()

        @pl.when(t == 3)
        def _():
            pass_extra.wait_recv()
            here = jnp.int32(1)
            for mask in (0, 1):
                again = repeats(lambda u: ids[mask, u, 0])
                for u in range(tiles):
                    here = jnp.where((again[u] == 1) & (ids[mask, u, 0] == col), 0, here)
            rows[3] = extra[here]

        @pl.when(t == 4)
        def _():
            give_diag.wait_recv()

        @pl.when(t == 1)
        def _():
            give_core.wait_recv()

        @pl.when(t < SLOTS)
        def _():
            compute(t)

        @pl.when(t == 0)
        def _():
            give_straight(0).wait_recv()
            pass_straight(0).start()
            give_second.wait_recv()
            mine = jnp.int32(1)
            for again in own_again:
                mine = jnp.where(again == 1, 0, mine)
            extra[0] = seconds[mine]
            give_extra.start()
            give_diag.start()
            for mask in (1, 2, 3):
                give_ids(mask).wait_recv()
            query_load.wait()
            swap.wait_recv()

        @pl.when(t == 1)
        def _():
            give_straight(1).wait_recv()
            pass_straight(1).start()

        @pl.when(t == z)
        def _():
            carry_on()

        @pl.when(t < heads // 2)
        def _():
            intra(2 * t)
            intra(2 * t + 1)

        @pl.when((t >= 3) & (t < SLOTS + 3))
        def _():
            take_far(t - 3)

        @pl.when((t >= 2) & (t < SLOTS + 2))
        def _():
            take_near(t - 2)

        @pl.when((t >= 1) & (t < SLOTS + 1))
        def _():
            take_x(t - 1)

        @pl.when(t == 2)
        def _():
            give_extra.wait_recv()
            pass_extra.start()

        @pl.when(t == 3)
        def _():
            join()

        @pl.when(t == 4)
        def _():
            finish()

        return carry

    lax.fori_loop(0, SLOTS + 3, step, 0)

    spilled, named = [], []
    for pair in ((0, 1), (2, 3)):
        total, expert = jnp.int32(0), jnp.int32(-1)
        for mask in pair:
            again = repeats(lambda u: ids[mask, u, 0])
            for u in range(tiles):
                total = total + again[u]
                expert = jnp.where(again[u] == 1, ids[mask, u, 0], expert)
        spilled.append(total)
        named.append(expert)
    both = jnp.where((spilled[0] == 1) & (spilled[1] == 1) & (named[0] == named[1]), 1, 0)
    spill_ref[0] = jnp.where((spilled[0] > 1) | (spilled[1] > 1), 1, both)

    swap.wait_send()

    @pl.when(z < PARTS - 1)
    def _():
        chain.wait_send()

    for j in (1, 2, 3):
        square(j).wait_send()
        give_ids(j).wait_send()
    for copy in (give_core, give_second, give_diag, give_extra, pass_extra):
        copy.wait_send()
    for i in range(2):
        give_straight(i).wait_send()
        pass_straight(i).wait_send()
    for t in range(SLOTS):
        for j in range(2):
            across(t, j).wait_send()
        along_near(t).wait_send()
        along_far(t).wait_send()
    for t, mask, slot in ((1, 1, 1), (2, 2, 2), (3, 1, 5), (3, 2, 6), (3, 3, 7), (4, 3, 3)):
        home(t, mask, slot).wait_send()
        home(t, mask, slot).wait_recv()
    for t in range(tiles):
        where = jnp.where(own_again[t] == 1, 4, 0)
        for mask in (1, 2, 3):
            where = where + jnp.where(ids_ref[t, 0] == flipped(col, mask), mask, 0)
        out_ref[t] = back[where]


def fast_call(row_tiles, tile_expert, w_gate, w_up, w_down, column_count, attention):
    tiles, tile_len, width = row_tiles.shape
    units = w_gate.shape[2]
    low, wide = jnp.bfloat16, jnp.float32
    block = (tile_len, column_count)
    tile = (tile_len, width)
    dma = pltpu.SemaphoreType.DMA
    queries, keys, values, gates, decay_rate, norm_gain = attention
    tokens, heads = queries.shape[0], decay_rate.shape[0]
    size = queries.shape[1] // heads
    vmem = pl.BlockSpec(memory_space=pltpu.VMEM)
    smem = pl.BlockSpec(memory_space=pltpu.SMEM)
    states = (heads, size, size)
    return pl.pallas_call(
        fast_kernel,
        out_shape=(
            jax.ShapeDtypeStruct((tiles,) + block, low),
            jax.ShapeDtypeStruct(queries.shape, low),
            jax.ShapeDtypeStruct((1,), jnp.int32),
        ),
        in_specs=[smem] * 2 + [pl.BlockSpec(memory_space=pl.ANY)] * 9,
        out_specs=(vmem, vmem, smem),
        scratch_shapes=[
            pltpu.SMEM((4,) + tile_expert.shape, jnp.int32),
            pltpu.VMEM((tiles,) + tile, low),
            pltpu.VMEM((width, units), low),
            pltpu.VMEM((width, units), low),
            pltpu.VMEM((units, width), low),
            pltpu.VMEM(queries.shape, low),
            pltpu.VMEM(queries.shape, low),
            pltpu.VMEM(queries.shape, low),
            pltpu.VMEM(queries.shape, low),
            pltpu.VMEM((1, queries.shape[1]), wide),
            pltpu.VMEM((SLOTS,) + tile, low),
            pltpu.VMEM((tile_len // 2, width), low),
            pltpu.VMEM(tile, low),
            pltpu.VMEM(tile, low),
            pltpu.VMEM((2,) + tile, low),
            pltpu.VMEM((2,) + tile, low),
            pltpu.VMEM((tile_len, units), low),
            pltpu.VMEM((SLOTS, PARTS) + block, wide),
            pltpu.VMEM((SLOTS, PARTS) + block, low),
            pltpu.VMEM((SLOTS, PARTS) + block, low),
            pltpu.VMEM((SLOTS, 2) + block, low),
            pltpu.VMEM((SLOTS, 2) + block, low),
            pltpu.VMEM((SLOTS,) + block, low),
            pltpu.VMEM((SLOTS,) + block, low),
            pltpu.VMEM((SLOTS,) + block, low),
            pltpu.VMEM((8,) + block, low),
            pltpu.VMEM(queries.shape, wide),
            pltpu.VMEM(states, wide),
            pltpu.VMEM(states, low),
            pltpu.VMEM(states, low),
            pltpu.VMEM(states, low),
            pltpu.VMEM(states, low),
            pltpu.VMEM(states, wide),
            pltpu.VMEM((tokens, size), wide),
            pltpu.VMEM((4, tokens, size), wide),
            dma((13,)),
            dma((2, 12)),
            dma((2, SLOTS, 2)),
            dma((2, SLOTS)),
            dma((2, SLOTS)),
            dma((2, 8)),
            dma((2,)),
            dma((2,)),
            dma((2, 4)),
        ],
        compiler_params=pltpu.CompilerParams(
            collective_id=1, has_side_effects=True, vmem_limit_bytes=62 * 1024 * 1024
        ),
        cost_estimate=pl.CostEstimate(
            flops=6 * SLOTS * tile_len * width * units,
            bytes_accessed=30_000_000,
            transcendentals=0,
        ),
        name="five_slots",
    )(
        tile_expert, decay_rate, row_tiles, w_gate, w_up, w_down,
        queries, keys, values, gates, norm_gain[None, :],
    )


def expert_part(moe_rows, tile_expert, row_weight, w_gate, w_up, w_down, attention):
    tiles_here = tile_expert.shape[0]
    tile_len = moe_rows.shape[0] // tiles_here
    model_width = moe_rows.shape[1]
    column_count = model_width // lax.axis_size("ctx")
    row_tiles = moe_rows.reshape(tiles_here, tile_len, model_width)
    tile_ids = tile_expert[:, 0]
    expert_count = lax.axis_size("exp")
    capacity = max(2, tiles_here // 2)
    order = jnp.arange(tiles_here)
    before = (tile_ids[None, :] == tile_ids[:, None]) & (order[None, :] < order[:, None])
    ranks = jnp.sum(before.astype(jnp.int32), axis=1)
    peers = lax.axis_size("ctx")
    heads = attention[4].shape[0]
    fits = peers % 2 == 0 and peers <= 2 * CHUNKS - 2 and column_count % 128 == 0 and heads <= CHUNKS
    weights_of = row_weight.reshape(tiles_here, tile_len)[:, :, None]

    def weigh(found):
        return (found.astype(jnp.float32) * weights_of).astype(jnp.bfloat16)

    def every_slot():
        chunk = jnp.arange(CHUNKS)
        expert_of = flipped(lax.axis_index("exp"), chunk_mask(chunk))
        match = (tile_ids[None, :] == expert_of[:, None]) & (
            ranks[None, :] == chunk_slot(chunk)[:, None]
        )
        index = jnp.sum(match * order[None, :], axis=1).astype(jnp.int32)
        send_buffer = pick_tiles(row_tiles, index)
        gathered, _ = expert_call(
            send_buffer, w_gate, w_up, w_down, column_count, attention
        )
        return jnp.sum(
            jnp.where(
                match[:, :, None, None], gathered[:, None], jnp.zeros((), jnp.bfloat16)
            ).astype(jnp.float32),
            axis=0,
        )

    if expert_count == 4 and capacity == 2 and tiles_here == 4 and heads == 8 and peers == 8 and fits:
        found, attention_out, spilled = fast_call(
            row_tiles, tile_expert, w_gate, w_up, w_down, column_count, attention
        )
        moe_tiles = lax.cond(spilled[0] > 0, lambda: weigh(every_slot()), lambda: weigh(found))
        return (attention_out, moe_tiles.reshape(tiles_here * tile_len, column_count))

    attention_out = attention_part(*attention)
    owner_match = tile_ids[None, None, :] == jnp.arange(expert_count)[:, None, None]
    slot_match = ranks[None, None, :] == jnp.arange(capacity)[None, :, None]
    source = jnp.sum((owner_match & slot_match) * order[None, None, :], axis=2)
    returned = []
    for slot in range(capacity):
        send_buffer = jnp.stack(
            [
                lax.dynamic_index_in_dim(row_tiles, source[owner, slot], 0, keepdims=False)
                for owner in range(expert_count)
            ]
        )
        arrived = lax.all_to_all(send_buffer, "exp", split_axis=0, concat_axis=0, tiled=True)
        flat_rows = arrived.reshape(-1, model_width)
        gate_part = jnp.dot(flat_rows, w_gate[0], preferred_element_type=jnp.float32)
        up_part = jnp.dot(flat_rows, w_up[0], preferred_element_type=jnp.float32)
        hidden = (jax.nn.silu(gate_part) * up_part).astype(jnp.bfloat16)
        partial_out = jnp.dot(hidden, w_down[0], preferred_element_type=jnp.float32)
        summed = lax.psum_scatter(
            partial_out.astype(jnp.bfloat16), "ctx", scatter_dimension=1, tiled=True
        )
        result = summed.reshape(arrived.shape[:-1] + (column_count,))
        returned.append(
            lax.all_to_all(result, "exp", split_axis=0, concat_axis=0, tiled=True)
        )
    gathered = jnp.stack(returned, axis=1)
    select = (owner_match & slot_match)[:, :, :, None, None]
    expert_out = jnp.sum(
        jnp.where(select, gathered[:, :, None], jnp.zeros((), jnp.bfloat16)).astype(jnp.float32),
        axis=(0, 1),
    )
    moe_out = weigh(expert_out).reshape(tiles_here * tile_len, column_count)
    return (attention_out, moe_out)


def on_device(
    queries,
    keys,
    values,
    gates,
    decay_rate,
    norm_gain,
    moe_rows,
    tile_expert,
    row_weight,
    w_gate,
    w_up,
    w_down,
):
    attention = (queries, keys, values, gates, decay_rate, norm_gain)
    return expert_part(moe_rows, tile_expert, row_weight, w_gate, w_up, w_down, attention)


def solution(mesh):
    placed = (
        P("ctx", "exp"),
        P("ctx", "exp"),
        P("ctx", "exp"),
        P("ctx", "exp"),
        P("exp"),
        P("exp"),
        P("exp", None),
        P("exp", None),
        P("exp"),
        P("exp", None, "ctx"),
        P("exp", None, "ctx"),
        P("exp", "ctx", None),
    )
    return jax.shard_map(
        on_device,
        mesh=mesh,
        in_specs=placed,
        out_specs=(P("ctx", "exp"), P("exp", "ctx")),
        check_vma=False,
    )
```

```python
import functools

import jax
import jax.numpy as jnp
from jax import lax
from jax.experimental import pallas as pl
from jax.experimental.pallas import tpu as pltpu
from jax.sharding import PartitionSpec as P

MESH = pl.DeviceIdType.MESH
CHUNKS = 8


def carried_state(local_state, decay_rate, tokens_here):
    peers, mine = (lax.axis_size("ctx"), lax.axis_index("ctx"))
    everything = lax.all_gather(local_state.astype(jnp.bfloat16), "ctx")
    distance = (mine - 1 - jnp.arange(peers)).astype(jnp.float32)
    weight = jnp.exp(-decay_rate[None, :] * tokens_here * jnp.maximum(distance, 0.0)[:, None])
    weight = jnp.where((distance >= 0.0)[:, None], weight, 0.0)
    return jnp.sum(everything.astype(jnp.float32) * weight[:, :, None, None], axis=0)


def attention_part(queries, keys, values, gates, decay_rate, norm_gain):
    tokens_here = queries.shape[0]
    heads_here = decay_rate.shape[0]
    head_width = queries.shape[1] // heads_here
    query_heads = queries.reshape(tokens_here, heads_here, head_width)
    key_heads = keys.reshape(tokens_here, heads_here, head_width)
    value_heads = values.reshape(tokens_here, heads_here, head_width)
    positions = jnp.arange(tokens_here, dtype=jnp.float32)
    offsets = positions[:, None] - positions[None, :]
    within = jnp.exp(-decay_rate[:, None, None] * jnp.maximum(offsets, 0.0)[None])
    within = jnp.where((offsets >= 0.0)[None], within, 0.0)
    query_decay = jnp.exp(-decay_rate[None, :] * positions[:, None])
    key_decay = jnp.exp(-decay_rate[None, :] * (tokens_here - positions)[:, None])
    key_scaled = (key_heads.astype(jnp.float32) * key_decay[:, :, None]).astype(jnp.bfloat16)
    local_state = jnp.einsum(
        "the,thf->hef", key_scaled, value_heads, preferred_element_type=jnp.float32
    )
    prefix = carried_state(local_state, decay_rate, tokens_here)
    scores = jnp.einsum("the,she->hts", query_heads, key_heads, preferred_element_type=jnp.float32)
    scores = (scores * within).astype(jnp.bfloat16)
    intra = jnp.einsum("hts,she->the", scores, value_heads, preferred_element_type=jnp.float32)
    inter = jnp.einsum(
        "the,hef->thf", query_heads, prefix.astype(jnp.bfloat16), preferred_element_type=jnp.float32
    )
    mixed = (intra + inter * query_decay[:, :, None]).reshape(tokens_here, heads_here * head_width)
    square_part = jnp.sum(mixed * mixed, axis=1)
    square_total = lax.psum(square_part, "exp")
    mean_square = square_total / (heads_here * head_width * lax.axis_size("exp"))
    scaled = mixed * lax.rsqrt(mean_square + 1e-06)[:, None] * norm_gain[None, :]
    return (scaled * jax.nn.sigmoid(gates.astype(jnp.float32))).astype(jnp.bfloat16)


def chunk_mask(t):
    late = t // 4
    return (1 - late) * (t // 2) + late * (2 + t % 2)


def chunk_slot(t):
    late = t // 4
    return (1 - late) * (t % 2) + late * ((t - 4) // 2)


def flipped(me, mask):
    low, high = me % 2, (me // 2) % 2
    return me + (mask % 2) * (1 - 2 * low) + 2 * (mask // 2) * (1 - 2 * high)


def pick_kernel(index_ref, tile_ref, out_ref):
    out_ref[...] = tile_ref[...]


def pick_tiles(row_tiles, index):
    tile_len, width = row_tiles.shape[1:]
    return pl.pallas_call(
        pick_kernel,
        grid_spec=pltpu.PrefetchScalarGridSpec(
            num_scalar_prefetch=1,
            grid=(CHUNKS,),
            in_specs=[pl.BlockSpec((1, tile_len, width), lambda t, index: (index[t], 0, 0))],
            out_specs=pl.BlockSpec((1, tile_len, width), lambda t, index: (t, 0, 0)),
        ),
        out_shape=jax.ShapeDtypeStruct((CHUNKS, tile_len, width), row_tiles.dtype),
        name="pick_tiles",
    )(index, row_tiles)


def expert_kernel(
    groups,
    send_ref,
    gate_hbm,
    up_hbm,
    down_hbm,
    rate_ref,
    query_ref,
    key_ref,
    value_ref,
    gates_ref,
    gain_ref,
    out_ref,
    mixed_ref,
    gate_w,
    up_w,
    down_w,
    arrived,
    hidden,
    kept,
    pair_out,
    pair_in,
    group_out,
    group_in,
    result,
    back,
    weight_sem,
    own_sem,
    give_send,
    give_recv,
    pair_send,
    pair_recv,
    group_send,
    group_recv,
    back_send,
    back_recv,
    mixed,
    state,
    state_out,
    state_in,
    chain_out,
    chain_in,
    prefix,
    square_out,
    square_in,
    state_sem,
    chain_sem,
    square_send,
    square_recv,
):
    row, col = lax.axis_index("ctx"), lax.axis_index("exp")
    half, group = row % 2, row // 2
    partner = row + 1 - 2 * half
    wide = kept.shape[-1]
    peers = [(row, flipped(col, mask)) for mask in (1, 2, 3)] + [(partner, col)]
    peers += [(((group + j) % groups) * 2 + half, col) for j in range(1, groups)]

    weights = [
        pltpu.make_async_copy(gate_hbm.at[0], gate_w, weight_sem.at[0]),
        pltpu.make_async_copy(up_hbm.at[0], up_w, weight_sem.at[1]),
        pltpu.make_async_copy(down_hbm.at[0], down_w, weight_sem.at[2]),
    ]
    own = [
        pltpu.make_async_copy(send_ref.at[t], arrived.at[t], own_sem.at[t]) for t in range(2)
    ]

    barrier = pltpu.get_barrier_semaphore()
    for peer in peers:
        pl.semaphore_signal(barrier, inc=1, device_id=peer, device_id_type=MESH)
    for copy in own + weights:
        copy.start()
    pl.semaphore_wait(barrier, len(peers))

    def give(t):
        return pltpu.make_async_remote_copy(
            src_ref=send_ref.at[t],
            dst_ref=arrived.at[t],
            send_sem=give_send.at[t],
            recv_sem=give_recv.at[t],
            device_id=(row, flipped(col, chunk_mask(t))),
            device_id_type=MESH,
        )

    def pair(t):
        return pltpu.make_async_remote_copy(
            src_ref=pair_out.at[t],
            dst_ref=pair_in.at[t],
            send_sem=pair_send.at[t],
            recv_sem=pair_recv.at[t],
            device_id=(partner, col),
            device_id_type=MESH,
        )

    def spread(t, j):
        target = (group + j) % groups
        return pltpu.make_async_remote_copy(
            src_ref=group_out.at[t, target],
            dst_ref=group_in.at[t, j],
            send_sem=group_send.at[t, j],
            recv_sem=group_recv.at[t, j],
            device_id=(target * 2 + half, col),
            device_id_type=MESH,
        )

    def home(t):
        return pltpu.make_async_remote_copy(
            src_ref=result.at[t],
            dst_ref=back.at[t],
            send_sem=back_send.at[t],
            recv_sem=back_recv.at[t],
            device_id=(row, flipped(col, chunk_mask(t))),
            device_id_type=MESH,
        )

    for t in (2, 3, 4, 5, 6, 7):
        give(t).start()

    tokens, features = query_ref.shape
    heads, size = state.shape[0], state.shape[1]
    place = lax.broadcasted_iota(jnp.int32, (tokens, size), 0).astype(jnp.float32)

    def lanes(h):
        return pl.ds(pl.multiple_of(h * size, 128), size)

    def fill(value):
        return jnp.exp(jnp.full((size, size), value, jnp.float32))

    swap = pltpu.make_async_remote_copy(
        src_ref=state_out,
        dst_ref=state_in,
        send_sem=state_sem.at[0],
        recv_sem=state_sem.at[1],
        device_id=(partner, col),
        device_id_type=MESH,
    )
    chain = pltpu.make_async_remote_copy(
        src_ref=chain_out,
        dst_ref=chain_in,
        send_sem=chain_sem.at[0],
        recv_sem=chain_sem.at[1],
        device_id=(((group + 1) % groups) * 2 + half, col),
        device_id_type=MESH,
    )

    def square(j):
        return pltpu.make_async_remote_copy(
            src_ref=square_out,
            dst_ref=square_in.at[j],
            send_sem=square_send.at[j],
            recv_sem=square_recv.at[j],
            device_id=(row, flipped(col, j)),
            device_id_type=MESH,
        )

    def local(h, carry):
        decay = jnp.exp(-rate_ref[h] * (tokens - place))
        scaled = (key_ref[:, lanes(h)].astype(jnp.float32) * decay).astype(jnp.bfloat16)
        found = lax.dot_general(
            scaled,
            value_ref[:, lanes(h)],
            (((0,), (0,)), ((), ())),
            preferred_element_type=jnp.float32,
        )
        state[h] = found
        state_out[h] = found.astype(jnp.bfloat16)
        return carry

    lax.fori_loop(0, heads, local, 0)
    swap.start()

    def intra(h):
        offset = lax.broadcasted_iota(jnp.int32, (tokens, tokens), 0) - lax.broadcasted_iota(
            jnp.int32, (tokens, tokens), 1
        )
        gap = jnp.maximum(offset, 0).astype(jnp.float32)
        within = jnp.where(offset >= 0, jnp.exp(-rate_ref[h] * gap), 0.0)
        scores = lax.dot_general(
            query_ref[:, lanes(h)],
            key_ref[:, lanes(h)],
            (((1,), (1,)), ((), ())),
            preferred_element_type=jnp.float32,
        )
        scores = (scores * within).astype(jnp.bfloat16)
        mixed[:, lanes(h)] = jnp.dot(
            scores, value_ref[:, lanes(h)], preferred_element_type=jnp.float32
        )

    def carry_on():
        @pl.when(group > 0)
        def _():
            chain.wait_recv()

        @pl.when(group == 0)
        def _():
            prefix[...] = jnp.zeros_like(prefix)

        @pl.when(group > 0)
        def _():
            prefix[...] = chain_in[...].astype(jnp.float32)

        first = (half == 0).astype(jnp.float32)

        def one(h, carry):
            decay = fill(-rate_ref[h] * tokens)
            mine, other, before = state[h], state_in[h].astype(jnp.float32), prefix[h]
            early = first * mine + (1.0 - first) * other
            late = first * other + (1.0 - first) * mine
            middle = before * decay + early
            chain_out[h] = (middle * decay + late).astype(jnp.bfloat16)
            prefix[h] = first * before + (1.0 - first) * middle
            return carry

        lax.fori_loop(0, heads, one, 0)

        @pl.when(group < groups - 1)
        def _():
            chain.start()

    def join():
        squares = jnp.zeros((tokens, size), jnp.float32)
        for h in range(heads):
            cut = slice(h * size, (h + 1) * size)
            inter = jnp.dot(
                query_ref[:, cut],
                prefix[h].astype(jnp.bfloat16),
                preferred_element_type=jnp.float32,
            )
            both = mixed[:, cut] + inter * jnp.exp(-rate_ref[h] * place)
            mixed[:, cut] = both
            squares = squares + both * both
        square_out[...] = squares
        for j in (1, 2, 3):
            square(j).start()

    for copy in own + weights:
        copy.wait()

    def step(t, carry):
        @pl.when(t < CHUNKS)
        def _():
            @pl.when(t >= 2)
            def _():
                give(t).wait_recv()

            span = 384 if hidden.shape[1] % 384 == 0 else 128
            for start in range(0, hidden.shape[1], span):
                cut = pl.ds(start, span)
                rows = arrived[t]
                gated = jnp.dot(rows, gate_w[:, cut], preferred_element_type=jnp.float32)
                raised = jnp.dot(rows, up_w[:, cut], preferred_element_type=jnp.float32)
                hidden[:, cut] = (jax.nn.silu(gated) * raised).astype(jnp.bfloat16)
            for g in range(groups):
                theirs = pl.ds(pl.multiple_of((2 * g + 1 - half) * wide, 128), wide)
                pair_out[t, g] = jnp.dot(
                    hidden[...], down_w[:, theirs], preferred_element_type=jnp.float32
                ).astype(jnp.bfloat16)
            pair(t).start()

            @pl.when(t < heads)
            def _():
                intra(t)

            for g in range(groups):
                mine = pl.ds(pl.multiple_of((2 * g + half) * wide, 128), wide)
                kept[t, g] = jnp.dot(
                    hidden[...], down_w[:, mine], preferred_element_type=jnp.float32
                )

        @pl.when((t >= 1) & (t < CHUNKS + 1))
        def _():
            u = t - 1
            pair(u).wait_recv()
            for g in range(groups):
                total = kept[u, g] + pair_in[u, g].astype(jnp.float32)
                kept[u, g] = total
                group_out[u, g] = total.astype(jnp.bfloat16)
            for j in range(1, groups):
                spread(u, j).start()

        @pl.when(t == 1)
        def _():
            swap.wait_recv()

        @pl.when(t == 1 + group)
        def _():
            carry_on()

        @pl.when(t == CHUNKS)
        def _():
            join()

        @pl.when(t >= 2)
        def _():
            u = t - 2
            total = kept[u, group]
            for j in range(1, groups):
                spread(u, j).wait_recv()
                total = total + group_in[u, j].astype(jnp.float32)
            result[u] = total.astype(jnp.bfloat16)

            @pl.when(u >= 2)
            def _():
                home(u).start()

        return carry

    lax.fori_loop(0, CHUNKS + 2, step, 0)

    squares = square_out[...]
    for j in (1, 2, 3):
        square(j).wait_recv()
        squares = squares + square_in[j]
    mean = jnp.sum(squares, axis=1, keepdims=True) / (features * 4)
    scale = lax.rsqrt(mean + 1e-06)
    for h in range(heads):
        cut = slice(h * size, (h + 1) * size)
        gate = jax.nn.sigmoid(gates_ref[:, cut].astype(jnp.float32))
        mixed_ref[:, cut] = (mixed[:, cut] * scale * gain_ref[:, cut] * gate).astype(jnp.bfloat16)
    swap.wait_send()

    @pl.when(group < groups - 1)
    def _():
        chain.wait_send()

    for j in (1, 2, 3):
        square(j).wait_send()
    for t in range(2):
        out_ref[t] = result[t]
    for t in range(CHUNKS):
        pair(t).wait_send()
        for j in range(1, groups):
            spread(t, j).wait_send()
    for t in range(2, CHUNKS):
        give(t).wait_send()
        home(t).wait_send()
        home(t).wait_recv()
        out_ref[t] = back[t]


def expert_call(send_buffer, w_gate, w_up, w_down, column_count, attention):
    tile_len, width = send_buffer.shape[1:]
    units = w_gate.shape[2]
    groups = lax.axis_size("ctx") // 2
    low, wide = jnp.bfloat16, jnp.float32
    block = (tile_len, column_count)
    dma = pltpu.SemaphoreType.DMA
    queries, keys, values, gates, decay_rate, norm_gain = attention
    tokens, heads = queries.shape[0], decay_rate.shape[0]
    size = queries.shape[1] // heads
    vmem = pl.BlockSpec(memory_space=pltpu.VMEM)
    return pl.pallas_call(
        functools.partial(expert_kernel, groups),
        out_shape=(
            jax.ShapeDtypeStruct((CHUNKS,) + block, low),
            jax.ShapeDtypeStruct(queries.shape, low),
        ),
        in_specs=[pl.BlockSpec(memory_space=pl.ANY)] * 4
        + [pl.BlockSpec(memory_space=pltpu.SMEM)]
        + [vmem] * 5,
        out_specs=(vmem, vmem),
        scratch_shapes=[
            pltpu.VMEM((width, units), low),
            pltpu.VMEM((width, units), low),
            pltpu.VMEM((units, width), low),
            pltpu.VMEM((CHUNKS, tile_len, width), low),
            pltpu.VMEM((tile_len, units), low),
            pltpu.VMEM((CHUNKS, groups) + block, wide),
            pltpu.VMEM((CHUNKS, groups) + block, low),
            pltpu.VMEM((CHUNKS, groups) + block, low),
            pltpu.VMEM((CHUNKS, groups) + block, low),
            pltpu.VMEM((CHUNKS, groups) + block, low),
            pltpu.VMEM((CHUNKS,) + block, low),
            pltpu.VMEM((CHUNKS,) + block, low),
            dma((3,)),
            dma((2,)),
            dma((CHUNKS,)),
            dma((CHUNKS,)),
            dma((CHUNKS,)),
            dma((CHUNKS,)),
            dma((CHUNKS, groups)),
            dma((CHUNKS, groups)),
            dma((CHUNKS,)),
            dma((CHUNKS,)),
            pltpu.VMEM(queries.shape, wide),
            pltpu.VMEM((heads, size, size), wide),
            pltpu.VMEM((heads, size, size), low),
            pltpu.VMEM((heads, size, size), low),
            pltpu.VMEM((heads, size, size), low),
            pltpu.VMEM((heads, size, size), low),
            pltpu.VMEM((heads, size, size), wide),
            pltpu.VMEM((tokens, size), wide),
            pltpu.VMEM((4, tokens, size), wide),
            dma((2,)),
            dma((2,)),
            dma((4,)),
            dma((4,)),
        ],
        compiler_params=pltpu.CompilerParams(
            collective_id=0, has_side_effects=True, vmem_limit_bytes=62 * 1024 * 1024
        ),
        cost_estimate=pl.CostEstimate(
            flops=6 * CHUNKS * tile_len * width * units,
            bytes_accessed=300_000_000,
            transcendentals=0,
        ),
        name="expert_tiles",
    )(
        send_buffer, w_gate, w_up, w_down,
        decay_rate, queries, keys, values, gates, norm_gain[None, :],
    )


SLOTS = 5
LAST = SLOTS - 1
PARTS = 4


def fast_kernel(
    ids_ref,
    rate_ref,
    rows_hbm,
    gate_hbm,
    up_hbm,
    down_hbm,
    query_hbm,
    key_hbm,
    value_hbm,
    gates_hbm,
    gain_hbm,
    out_ref,
    mixed_ref,
    spill_ref,
    ids,
    raw,
    gate_w,
    up_w,
    down_w,
    query,
    key,
    value,
    gates,
    gain,
    rows,
    straight_out,
    core_out,
    diag_out,
    seconds,
    extra,
    halves_out,
    halves,
    hidden,
    kept,
    x_out,
    x_in,
    near_out,
    near_in,
    far_out,
    far_in,
    result,
    back,
    mixed,
    state,
    state_out,
    state_in,
    chain_out,
    chain_in,
    prefix,
    square_out,
    square_in,
    load_sem,
    give_sem,
    x_sem,
    near_sem,
    far_sem,
    home_sem,
    state_sem,
    chain_sem,
    square_sem,
    hello_sem,
):
    row, col = lax.axis_index("ctx"), lax.axis_index("exp")
    half, z = row % 2, row // 2
    core, odd = col % 2, z % 2
    partner = row + 1 - 2 * half
    near = z + 1 - 2 * odd
    far, cross = (z + 2) % PARTS, (near + 2) % PARTS
    order = (cross, near, far, z)
    tiles, tile_len = raw.shape[0], raw.shape[1]
    wide = kept.shape[-1]
    units = hidden.shape[1]
    span = units // 3
    half_len, piece = tile_len // 2, tile_len // 4

    def line(other):
        return (other * 2 + half, col)

    def mate(mask):
        return (row, flipped(col, mask))

    def load(source, target, number):
        return pltpu.make_async_copy(source, target, load_sem.at[number])

    def weight_cut(number):
        cut = pl.ds(number * span, span)
        return [
            load(gate_hbm.at[0, :, cut], gate_w.at[:, cut], 4 + 2 * number),
            load(up_hbm.at[0, :, cut], up_w.at[:, cut], 5 + 2 * number),
        ]

    key_load, value_load = load(key_hbm, key, 0), load(value_hbm, value, 1)
    query_load, rows_load = load(query_hbm, query, 2), load(rows_hbm, raw, 3)
    down_load = load(down_hbm.at[0], down_w, 10)
    gates_load, gain_load = load(gates_hbm, gates, 11), load(gain_hbm, gain, 12)

    peers = [mate(mask) for mask in (1, 2, 3)] + [(partner, col), line(near)]
    inner = ((z + 1) // 2) % 2
    barrier = pltpu.get_barrier_semaphore()
    for peer in peers:
        pl.semaphore_signal(barrier, inc=1, device_id=peer, device_id_type=MESH)

    @pl.when(inner == 1)
    def _():
        pl.semaphore_signal(barrier, inc=1, device_id=line(cross), device_id_type=MESH)

    for copy in [key_load, value_load, rows_load] + weight_cut(0) + weight_cut(1) + weight_cut(2):
        copy.start()
    for copy in (down_load, query_load, gates_load, gain_load):
        copy.start()

    def remote(source, target, sems, place, device):
        return pltpu.make_async_remote_copy(
            src_ref=source,
            dst_ref=target,
            send_sem=sems.at[(0,) + place],
            recv_sem=sems.at[(1,) + place],
            device_id=device,
            device_id_type=MESH,
        )

    my_core = pl.ds(pl.multiple_of(core * half_len, 32), half_len)
    other_core = pl.ds(pl.multiple_of((1 - core) * half_len, 32), half_len)

    def my_piece(i):
        return pl.ds(pl.multiple_of(odd * half_len + i * piece, 32), piece)

    def give_ids(mask):
        return remote(ids_ref, ids.at[mask], give_sem, (8 + mask,), mate(mask))

    give_core = remote(core_out, rows.at[1], give_sem, (0,), mate(1))
    give_second = remote(seconds.at[0], seconds.at[1], give_sem, (1,), mate(1))
    give_diag = remote(diag_out, rows.at[3], give_sem, (8,), mate(3))
    give_extra = remote(
        extra.at[0, my_core], extra.at[1, my_core], give_sem, (6,), mate(2)
    )
    pass_extra = remote(
        extra.at[1, my_core], extra.at[1, my_core], give_sem, (7,), mate(1)
    )

    def give_straight(i):
        return remote(
            straight_out.at[pl.ds(i * piece, piece)],
            rows.at[2, my_piece(i)],
            give_sem,
            (2 + i,),
            mate(2),
        )

    def pass_straight(i):
        return remote(
            rows.at[2, my_piece(i)], rows.at[2, my_piece(i)], give_sem, (4 + i,), line(near)
        )

    def length(t):
        return half_len if isinstance(t, int) and t == LAST else tile_len

    def across(t, j):
        cut, long = pl.ds(2 * j, 2), pl.ds(0, length(t))
        return remote(
            x_out.at[t, cut, long], x_in.at[t, cut, long], x_sem, (t, j), (partner, col)
        )

    def along_near(t):
        long = pl.ds(0, length(t))
        return remote(near_out.at[t, :, long], near_in.at[t, :, long], near_sem, (t,), line(near))

    def along_far(t):
        long = pl.ds(0, length(t))
        return remote(far_out.at[t, long], far_in.at[t, long], far_sem, (t,), line(far))

    def home(t, mask):
        return remote(result.at[t], back.at[mask], home_sem, (mask,), mate(mask))

    def home_extra(mask):
        return remote(
            result.at[LAST, pl.ds(0, half_len)],
            back.at[4 + mask // 2, my_core],
            home_sem,
            (4 + mask,),
            mate(mask),
        )

    def swap_halves(j):
        cut = pl.ds(4 * j, 4)
        return remote(halves_out.at[cut], halves.at[1, cut], give_sem, (12 + j,), mate(1))

    swap = remote(state_out, state_in, state_sem, (), (partner, col))
    chain = remote(chain_out, chain_in, chain_sem, (), line((z + 1) % PARTS))

    def square(j):
        return remote(square_out, square_in.at[j], square_sem, (j,), mate(j))

    def first_of(expert):
        found = jnp.int32(0)
        for t in reversed(range(tiles)):
            found = jnp.where(ids_ref[0, t] == expert, t, found)
        return found

    def repeats(read):
        seen = []
        for t in range(tiles):
            again = jnp.int32(0)
            for u in range(t):
                again = jnp.where(read(u) == read(t), 1, again)
            seen.append(again)
        return seen

    own_again = repeats(lambda t: ids_ref[0, t])

    tokens, features = query.shape
    heads, size = state.shape[0], state.shape[1]
    place = lax.broadcasted_iota(jnp.int32, (tokens, size), 0).astype(jnp.float32)

    def lanes(h):
        return pl.ds(pl.multiple_of(h * size, 128), size)

    def fill(number):
        return jnp.exp(jnp.full((size, size), number, jnp.float32))

    key_load.wait()
    value_load.wait()

    def local(h, carry):
        decay = jnp.exp(-rate_ref[h] * (tokens - place))
        scaled = (key[:, lanes(h)].astype(jnp.float32) * decay).astype(jnp.bfloat16)
        found = lax.dot_general(
            scaled,
            value[:, lanes(h)],
            (((0,), (0,)), ((), ())),
            preferred_element_type=jnp.float32,
        )
        state[h] = found
        state_out[h] = found.astype(jnp.bfloat16)
        return carry

    lax.fori_loop(0, heads, local, 0)
    for t in range(tiles):
        ids[0, 0, t] = ids_ref[0, t]
    rows_load.wait()
    my_half = pl.ds(pl.multiple_of(odd * half_len, 32), half_len)
    straight_out[...] = raw[first_of(flipped(col, 2)), my_half, :]

    pl.semaphore_wait(barrier, len(peers) + inner)
    for i in range(2):
        give_straight(i).start()
    swap.start()
    core_out[...] = raw[first_of(flipped(col, 1))]
    give_core.start()
    second = jnp.int32(0)
    for t in range(tiles):
        second = jnp.where(own_again[t] == 1, t, second)
    seconds[0] = raw[second]
    give_second.start()
    for mask in (1, 2, 3):
        give_ids(mask).start()

    @pl.when(inner == 1)
    def _():
        pl.semaphore_signal(hello_sem, inc=1, device_id=line(cross), device_id_type=MESH)

    rows[0] = raw[first_of(col)]
    diag_out[...] = raw[first_of(flipped(col, 3))]

    def intra(h):
        offset = lax.broadcasted_iota(jnp.int32, (tokens, tokens), 0) - lax.broadcasted_iota(
            jnp.int32, (tokens, tokens), 1
        )
        gap = jnp.maximum(offset, 0).astype(jnp.float32)
        within = jnp.where(offset >= 0, jnp.exp(-rate_ref[h] * gap), 0.0)
        scores = lax.dot_general(
            query[:, lanes(h)],
            key[:, lanes(h)],
            (((1,), (1,)), ((), ())),
            preferred_element_type=jnp.float32,
        )
        scores = (scores * within).astype(jnp.bfloat16)
        mixed[:, lanes(h)] = jnp.dot(scores, value[:, lanes(h)], preferred_element_type=jnp.float32)

    def carry_on():
        @pl.when(z > 0)
        def _():
            chain.wait_recv()
            prefix[...] = chain_in[...].astype(jnp.float32)

        @pl.when(z == 0)
        def _():
            prefix[...] = jnp.zeros_like(prefix)

        first = (half == 0).astype(jnp.float32)

        def one(h, carry):
            decay = fill(-rate_ref[h] * tokens)
            mine, other, before = state[h], state_in[h].astype(jnp.float32), prefix[h]
            early = first * mine + (1.0 - first) * other
            late = first * other + (1.0 - first) * mine
            middle = before * decay + early
            chain_out[h] = (middle * decay + late).astype(jnp.bfloat16)
            prefix[h] = first * before + (1.0 - first) * middle
            return carry

        lax.fori_loop(0, heads, one, 0)

        @pl.when(z < PARTS - 1)
        def _():
            chain.start()

    def join():
        squares = jnp.zeros((tokens, size), jnp.float32)
        for h in range(heads):
            cut = slice(h * size, (h + 1) * size)
            inter = jnp.dot(
                query[:, cut], prefix[h].astype(jnp.bfloat16), preferred_element_type=jnp.float32
            )
            both = mixed[:, cut] + inter * jnp.exp(-rate_ref[h] * place)
            mixed[:, cut] = both
            squares = squares + both * both
        square_out[...] = lax.dot_general(
            jnp.ones((8, size), jnp.float32),
            squares,
            (((1,), (1,)), ((), ())),
            precision=lax.Precision.HIGHEST,
            preferred_element_type=jnp.float32,
        )
        for j in (1, 2, 3):
            square(j).start()

    def finish():
        gates_load.wait()
        gain_load.wait()
        squares = square_out[...]
        for j in (1, 2, 3):
            square(j).wait_recv()
            squares = squares + square_in[j]
        scale = lax.dot_general(
            lax.rsqrt(squares / (features * 4) + 1e-06),
            jnp.full((8, size), 0.125, jnp.float32),
            (((0,), (0,)), ((), ())),
            precision=lax.Precision.HIGHEST,
            preferred_element_type=jnp.float32,
        )
        for h in range(heads):
            cut = slice(h * size, (h + 1) * size)
            gate = jax.nn.sigmoid(gates[:, cut].astype(jnp.float32))
            mixed_ref[:, cut] = (mixed[:, cut] * scale * gain[:, cut] * gate).astype(jnp.bfloat16)

    def compute(t):
        for number in range(3):
            cut = pl.ds(number * span, span)

            @pl.when(t == 0)
            def _():
                for copy in weight_cut(number):
                    copy.wait()

            tile = rows[t]
            gated = jnp.dot(tile, gate_w[:, cut], preferred_element_type=jnp.float32)
            raised = jnp.dot(tile, up_w[:, cut], preferred_element_type=jnp.float32)
            hidden[:, cut] = (jax.nn.silu(gated) * raised).astype(jnp.bfloat16)

        @pl.when(t == 0)
        def _():
            down_load.wait()

    def block(part, side):
        cut = pl.ds(pl.multiple_of((2 * order[part] + side) * wide, 128), wide)
        return jnp.dot(hidden[...], down_w[:, cut], preferred_element_type=jnp.float32)

    def spread(t):
        for j in range(2):
            for part in (2 * j, 2 * j + 1):
                x_out[t, part] = block(part, 1 - half).astype(jnp.bfloat16)
            across(t, j).start()
        for part in range(PARTS):
            kept[t, part] = block(part, half)

    def spread_extra():
        for j in range(2):
            side = half if j else 1 - half
            for part in range(PARTS):
                found = block(part, side).astype(jnp.bfloat16)
                halves_out[4 * j + part] = found[:half_len]
                halves[0, 4 * j + part] = found[half_len:]
            swap_halves(j).start()
        theirs = jnp.int32(1)
        for mask in range(4):
            again = repeats(lambda u: ids[mask, 0, u])
            for u in range(tiles):
                theirs = jnp.where((again[u] == 1) & (ids[mask, 0, u] == col), 0, theirs)
        for j in range(2):
            swap_halves(j).wait_recv()
        for j in range(2):
            for part in (2 * j, 2 * j + 1):
                x_out[LAST, part, :half_len] = halves[theirs, part]
            across(LAST, j).start()
        for part in range(PARTS):
            kept[LAST, part, :half_len] = halves[theirs, 4 + part].astype(jnp.float32)

    def take_x(u, j):
        long = pl.ds(0, length(u))
        across(u, j).wait_recv()
        for part in (2 * j, 2 * j + 1):
            total = kept[u, part, long] + x_in[u, part, long].astype(jnp.float32)
            if j == 0:
                near_out[u, part, long] = total.astype(jnp.bfloat16)
            else:
                kept[u, part, long] = total
        if j == 0:
            along_near(u).start()

    def take_near(u):
        long = pl.ds(0, length(u))
        along_near(u).wait_recv()
        far_out[u, long] = (kept[u, 2, long] + near_in[u, 0, long].astype(jnp.float32)).astype(
            jnp.bfloat16
        )
        along_far(u).start()
        kept[u, 3, long] = kept[u, 3, long] + near_in[u, 1, long].astype(jnp.float32)

    def take_far(u):
        long = pl.ds(0, length(u))
        along_far(u).wait_recv()
        done = (kept[u, 3, long] + far_in[u, long].astype(jnp.float32)).astype(jnp.bfloat16)
        if isinstance(u, int) and u == LAST:
            result[u, long] = done
            for mask in (2, 3, 1):
                home_extra(mask).start()
            back[4, my_core] = done
        elif isinstance(u, int):
            result[u] = done
            home(u, u).start()
        else:
            result[u] = done
            for slot in range(1, LAST):

                @pl.when(u == slot)
                def _():
                    home(u, slot).start()

    def step(t, carry):
        @pl.when(t == 4)
        def _():
            join()

        @pl.when(t == 4)
        def _():
            take_x(3, 0)

        @pl.when(t == 1)
        def _():
            give_core.wait_recv()

        @pl.when(t == 2)
        def _():
            for i in range(2):
                pass_straight(i).wait_recv()

        @pl.when(t == 3)
        def _():
            give_diag.wait_recv()

        @pl.when(t == 4)
        def _():
            give_extra.wait_recv()
            pass_extra.start()
            here = jnp.int32(1)
            for mask in (0, 1):
                again = repeats(lambda u: ids[mask, 0, u])
                for u in range(tiles):
                    here = jnp.where((again[u] == 1) & (ids[mask, 0, u] == col), 0, here)
            pass_extra.wait_recv()
            rows[4, :half_len] = extra[here, other_core, :]
            rows[4, half_len:] = extra[here, my_core, :]

        compute(t)

        @pl.when(t < LAST)
        def _():
            spread(t)

        @pl.when(t == LAST)
        def _():
            spread_extra()

        @pl.when(t == 0)
        def _():
            give_straight(0).wait_recv()
            pass_straight(0).start()
            give_second.wait_recv()
            mine = jnp.int32(1)
            for again in own_again:
                mine = jnp.where(again == 1, 0, mine)
            extra[0] = seconds[mine]
            give_diag.start()
            give_extra.start()
            for mask in (1, 2, 3):
                give_ids(mask).wait_recv()
            query_load.wait()
            swap.wait_recv()

        @pl.when(t == 1)
        def _():
            give_straight(1).wait_recv()
            pass_straight(1).start()

        @pl.when(t < heads // 2)
        def _():
            intra(2 * t)
            intra(2 * t + 1)

        @pl.when((t == 2) & (inner == 1))
        def _():
            pl.semaphore_wait(hello_sem, 1)

        @pl.when(t == 2)
        def _():
            take_near(t - 2)

        @pl.when(t >= 3)
        def _():
            take_near(t - 2)
            take_far(t - 3)

        @pl.when((t >= 1) & (t < LAST))
        def _():
            take_x(t - 1, 0)
            take_x(t - 1, 1)

        @pl.when(t == z)
        def _():
            carry_on()

        return carry

    lax.fori_loop(0, SLOTS, step, 0)
    take_x(3, 1)
    take_near(3)
    take_far(2)
    finish()
    take_x(LAST, 0)
    take_far(3)
    take_x(LAST, 1)
    take_near(LAST)
    take_far(LAST)
    back[0] = result[0]

    spilled, named = [], []
    for pair in ((0, 1), (2, 3)):
        total, expert = jnp.int32(0), jnp.int32(-1)
        for mask in pair:
            again = repeats(lambda u: ids[mask, 0, u])
            for u in range(tiles):
                total = total + again[u]
                expert = jnp.where(again[u] == 1, ids[mask, 0, u], expert)
        spilled.append(total)
        named.append(expert)
    sides = [jnp.where(expert >= 2, 1, 0) for expert in named]
    both = jnp.where((spilled[0] == 1) & (spilled[1] == 1) & (sides[0] == sides[1]), 1, 0)
    spill_ref[0] = jnp.where((spilled[0] > 1) | (spilled[1] > 1), 1, both)

    swap.wait_send()

    @pl.when(z < PARTS - 1)
    def _():
        chain.wait_send()

    for j in (1, 2, 3):
        square(j).wait_send()
        give_ids(j).wait_send()
    for copy in (give_core, give_second, give_diag, give_extra, pass_extra):
        copy.wait_send()
    for i in range(2):
        give_straight(i).wait_send()
        pass_straight(i).wait_send()
    for t in range(SLOTS):
        for j in range(2):
            across(t, j).wait_send()
        along_near(t).wait_send()
        along_far(t).wait_send()
    for j in range(2):
        swap_halves(j).wait_send()
    for mask in (1, 2, 3):
        home(mask, mask).wait_send()
        home(mask, mask).wait_recv()
        home_extra(mask).wait_send()
        home_extra(mask).wait_recv()
    for t in range(tiles):
        where, side = jnp.int32(0), jnp.int32(4)
        for mask in (1, 2, 3):
            there = ids_ref[0, t] == flipped(col, mask)
            where = where + jnp.where(there, mask, 0)
            side = side + jnp.where(there, mask // 2, 0)
        out_ref[t] = back[jnp.where(own_again[t] == 1, side, where)]


def fast_call(row_tiles, tile_expert, w_gate, w_up, w_down, column_count, attention):
    tiles, tile_len, width = row_tiles.shape
    units = w_gate.shape[2]
    low, wide = jnp.bfloat16, jnp.float32
    block = (tile_len, column_count)
    tile = (tile_len, width)
    dma = pltpu.SemaphoreType.DMA
    queries, keys, values, gates, decay_rate, norm_gain = attention
    tokens, heads = queries.shape[0], decay_rate.shape[0]
    size = queries.shape[1] // heads
    vmem = pl.BlockSpec(memory_space=pltpu.VMEM)
    smem = pl.BlockSpec(memory_space=pltpu.SMEM)
    states = (heads, size, size)
    return pl.pallas_call(
        fast_kernel,
        out_shape=(
            jax.ShapeDtypeStruct((tiles,) + block, low),
            jax.ShapeDtypeStruct(queries.shape, low),
            jax.ShapeDtypeStruct((1,), jnp.int32),
        ),
        in_specs=[smem] * 2 + [pl.BlockSpec(memory_space=pl.ANY)] * 9,
        out_specs=(vmem, vmem, smem),
        scratch_shapes=[
            pltpu.SMEM((4, 1, tiles), jnp.int32),
            pltpu.VMEM((tiles,) + tile, low),
            pltpu.VMEM((width, units), low),
            pltpu.VMEM((width, units), low),
            pltpu.VMEM((units, width), low),
            pltpu.VMEM(queries.shape, low),
            pltpu.VMEM(queries.shape, low),
            pltpu.VMEM(queries.shape, low),
            pltpu.VMEM(queries.shape, low),
            pltpu.VMEM((1, queries.shape[1]), wide),
            pltpu.VMEM((SLOTS,) + tile, low),
            pltpu.VMEM((tile_len // 2, width), low),
            pltpu.VMEM(tile, low),
            pltpu.VMEM(tile, low),
            pltpu.VMEM((2,) + tile, low),
            pltpu.VMEM((2,) + tile, low),
            pltpu.VMEM((8, tile_len // 2, column_count), low),
            pltpu.VMEM((2, 8, tile_len // 2, column_count), low),
            pltpu.VMEM((tile_len, units), low),
            pltpu.VMEM((SLOTS, PARTS) + block, wide),
            pltpu.VMEM((SLOTS, PARTS) + block, low),
            pltpu.VMEM((SLOTS, PARTS) + block, low),
            pltpu.VMEM((SLOTS, 2) + block, low),
            pltpu.VMEM((SLOTS, 2) + block, low),
            pltpu.VMEM((SLOTS,) + block, low),
            pltpu.VMEM((SLOTS,) + block, low),
            pltpu.VMEM((SLOTS,) + block, low),
            pltpu.VMEM((6,) + block, low),
            pltpu.VMEM(queries.shape, wide),
            pltpu.VMEM(states, wide),
            pltpu.VMEM(states, low),
            pltpu.VMEM(states, low),
            pltpu.VMEM(states, low),
            pltpu.VMEM(states, low),
            pltpu.VMEM(states, wide),
            pltpu.VMEM((8, tokens), wide),
            pltpu.VMEM((4, 8, tokens), wide),
            dma((13,)),
            dma((2, 14)),
            dma((2, SLOTS, 2)),
            dma((2, SLOTS)),
            dma((2, SLOTS)),
            dma((2, 8)),
            dma((2,)),
            dma((2,)),
            dma((2, 4)),
            pltpu.SemaphoreType.REGULAR,
        ],
        compiler_params=pltpu.CompilerParams(
            collective_id=1, has_side_effects=True, vmem_limit_bytes=62 * 1024 * 1024
        ),
        cost_estimate=pl.CostEstimate(
            flops=6 * SLOTS * tile_len * width * units,
            bytes_accessed=30_000_000,
            transcendentals=0,
        ),
        name="five_slots",
    )(
        tile_expert.T, decay_rate, row_tiles, w_gate, w_up, w_down,
        queries, keys, values, gates, norm_gain[None, :],
    )


def expert_part(moe_rows, tile_expert, row_weight, w_gate, w_up, w_down, attention):
    tiles_here = tile_expert.shape[0]
    tile_len = moe_rows.shape[0] // tiles_here
    model_width = moe_rows.shape[1]
    column_count = model_width // lax.axis_size("ctx")
    row_tiles = moe_rows.reshape(tiles_here, tile_len, model_width)
    tile_ids = tile_expert[:, 0]
    expert_count = lax.axis_size("exp")
    capacity = max(2, tiles_here // 2)
    order = jnp.arange(tiles_here)
    before = (tile_ids[None, :] == tile_ids[:, None]) & (order[None, :] < order[:, None])
    ranks = jnp.sum(before.astype(jnp.int32), axis=1)
    peers = lax.axis_size("ctx")
    heads = attention[4].shape[0]
    fits = peers % 2 == 0 and peers <= 2 * CHUNKS - 2 and column_count % 128 == 0 and heads <= CHUNKS
    weights_of = row_weight.reshape(tiles_here, tile_len)[:, :, None]

    def weigh(found):
        return (found.astype(jnp.float32) * weights_of).astype(jnp.bfloat16)

    def every_slot():
        chunk = jnp.arange(CHUNKS)
        expert_of = flipped(lax.axis_index("exp"), chunk_mask(chunk))
        match = (tile_ids[None, :] == expert_of[:, None]) & (
            ranks[None, :] == chunk_slot(chunk)[:, None]
        )
        index = jnp.sum(match * order[None, :], axis=1).astype(jnp.int32)
        send_buffer = pick_tiles(row_tiles, index)
        gathered, _ = expert_call(
            send_buffer, w_gate, w_up, w_down, column_count, attention
        )
        return jnp.sum(
            jnp.where(
                match[:, :, None, None], gathered[:, None], jnp.zeros((), jnp.bfloat16)
            ).astype(jnp.float32),
            axis=0,
        )

    if expert_count == 4 and capacity == 2 and tiles_here == 4 and heads == 8 and peers == 8 and fits:
        found, attention_out, spilled = fast_call(
            row_tiles, tile_expert, w_gate, w_up, w_down, column_count, attention
        )
        moe_tiles = lax.cond(spilled[0] > 0, lambda: weigh(every_slot()), lambda: weigh(found))
        return (attention_out, moe_tiles.reshape(tiles_here * tile_len, column_count))

    attention_out = attention_part(*attention)
    owner_match = tile_ids[None, None, :] == jnp.arange(expert_count)[:, None, None]
    slot_match = ranks[None, None, :] == jnp.arange(capacity)[None, :, None]
    source = jnp.sum((owner_match & slot_match) * order[None, None, :], axis=2)
    returned = []
    for slot in range(capacity):
        send_buffer = jnp.stack(
            [
                lax.dynamic_index_in_dim(row_tiles, source[owner, slot], 0, keepdims=False)
                for owner in range(expert_count)
            ]
        )
        arrived = lax.all_to_all(send_buffer, "exp", split_axis=0, concat_axis=0, tiled=True)
        flat_rows = arrived.reshape(-1, model_width)
        gate_part = jnp.dot(flat_rows, w_gate[0], preferred_element_type=jnp.float32)
        up_part = jnp.dot(flat_rows, w_up[0], preferred_element_type=jnp.float32)
        hidden = (jax.nn.silu(gate_part) * up_part).astype(jnp.bfloat16)
        partial_out = jnp.dot(hidden, w_down[0], preferred_element_type=jnp.float32)
        summed = lax.psum_scatter(
            partial_out.astype(jnp.bfloat16), "ctx", scatter_dimension=1, tiled=True
        )
        result = summed.reshape(arrived.shape[:-1] + (column_count,))
        returned.append(
            lax.all_to_all(result, "exp", split_axis=0, concat_axis=0, tiled=True)
        )
    gathered = jnp.stack(returned, axis=1)
    select = (owner_match & slot_match)[:, :, :, None, None]
    expert_out = jnp.sum(
        jnp.where(select, gathered[:, :, None], jnp.zeros((), jnp.bfloat16)).astype(jnp.float32),
        axis=(0, 1),
    )
    moe_out = weigh(expert_out).reshape(tiles_here * tile_len, column_count)
    return (attention_out, moe_out)


def on_device(
    queries,
    keys,
    values,
    gates,
    decay_rate,
    norm_gain,
    moe_rows,
    tile_expert,
    row_weight,
    w_gate,
    w_up,
    w_down,
):
    attention = (queries, keys, values, gates, decay_rate, norm_gain)
    return expert_part(moe_rows, tile_expert, row_weight, w_gate, w_up, w_down, attention)


def solution(mesh):
    placed = (
        P("ctx", "exp"),
        P("ctx", "exp"),
        P("ctx", "exp"),
        P("ctx", "exp"),
        P("exp"),
        P("exp"),
        P("exp", None),
        P("exp", None),
        P("exp"),
        P("exp", None, "ctx"),
        P("exp", None, "ctx"),
        P("exp", "ctx", None),
    )
    return jax.shard_map(
        on_device,
        mesh=mesh,
        in_specs=placed,
        out_specs=(P("ctx", "exp"), P("exp", "ctx")),
        check_vma=False,
    )
```
